32 devices in a mesh: tok: 2 (over core), head: 4 (over y, x), exp: 4 (over z).
Axes of the slice: x: 2, y: 2, z: 4, core: 2. Of those that a mesh axis runs over, the one named last changes fastest.
Arguments:
- context: bfloat16 [4, 64, 4096], P('exp', 'tok', 'head'), may hold values from -6 to 6
- out_proj: bfloat16 [4096, 4096], P('head', 'exp'), may hold values from -0.125 to 0.125
- stream: float32 [4, 64, 4096], P('exp', 'tok', 'head'), may hold values from -75 to 75
- norm_gain: float32 [4096], replicated, may hold values from 0.1 to 1.9
- expert_ids: int32 [4, 64, 8], P('exp', 'tok'), may hold values from 0 to 31, as said below
- slot_ids: int32 [4, 64, 8], P('exp', 'tok'), may hold values from -1 to 11, as said below
- gate_probs: float32 [4, 64, 8], P('exp', 'tok'), may hold values from 0.02 to 0.3
- w_gate: bfloat16 [32, 3072, 4096], P(('tok', 'exp'), 'head'), may hold values from -0.09375 to 0.09375
- w_up: bfloat16 [32, 3072, 4096], P(('tok', 'exp'), 'head'), may hold values from -0.09375 to 0.09375
- w_down: bfloat16 [32, 3072, 4096], P(('tok', 'exp'), 'head'), may hold values from -0.15625 to 0.15625
Outputs:
- mixed: float32 [4, 64, 4096], P('exp', 'tok', 'head')
The draws below stay inside these ranges and needn't reach their ends.
Inputs may be any that keep to these rules, and one draw needn't show every extreme that they name: `expert_ids`: each token names 8 different experts. `slot_ids`: within a block of 32 consecutive tokens of one image, the choices of one expert take slots 0, 1, 2, ... in token order until its 12 slots are full, later ones get -1; in every block some expert fills all 12 slots.
All inputs are finite; a program needn't handle non-finite values.
Results may differ from the reference program's by a relative error of at most 0.0034.
Values may be sent and summed in bfloat16 or wider, within the bound.
A program may use at most 128 MiB of HBM per device.

```python
import jax
import jax.numpy as jnp
from jax import lax

D = 4096
HID = 3072
EXPERTS = 32
TOP = 8
TOK_DEV = 32
CAP = 12
IMAGES = 4
SEQ = 64
N_HEAD = 4


def routing_table(key):
    base_key = jax.random.fold_in(key, 4242)
    key_pop, key_noise, key_hot, key_rows = jax.random.split(base_key, 4)
    block_count = IMAGES * SEQ // TOK_DEV
    popular = jax.random.randint(key_pop, (EXPERTS,), 0, 64) ** 2
    noise = jax.random.randint(key_noise, (block_count, TOK_DEV, EXPERTS), 0, 4096)
    hot_expert = jax.random.randint(key_hot, (), 0, EXPERTS)
    row_keys = jax.random.split(key_rows, block_count)
    orders = jax.vmap(lambda one_key: jax.random.permutation(one_key, TOK_DEV))(row_keys)
    places = jnp.argsort(orders, axis=1, stable=True)
    forced = (places < CAP).astype(jnp.int32)
    expert_range = jnp.arange(EXPERTS, dtype=jnp.int32)
    is_hot = (expert_range == hot_expert).astype(jnp.int32)
    score = noise + popular[None, None, :] + forced[:, :, None] * is_hot[None, None, :] * 1048576
    distinct = score * EXPERTS + expert_range[None, None, :]
    chosen = lax.top_k(distinct, TOP)[1].astype(jnp.int32)
    one_hot = jnp.sum((chosen[:, :, :, None] == expert_range).astype(jnp.int32), axis=2)
    before = jnp.cumsum(one_hot, axis=1) - one_hot
    ranked = jnp.take_along_axis(before, chosen, axis=2)
    slots = jnp.where(ranked < CAP, ranked, -1).astype(jnp.int32)
    return (chosen.reshape(IMAGES, SEQ, TOP), slots.reshape(IMAGES, SEQ, TOP))


def draw_expert_ids(key, part):
    return routing_table(key)[0]


def draw_slot_ids(key, part):
    return routing_table(key)[1]


def draw_stream(key, part):
    key_base, key_cols, key_rows = jax.random.split(jax.random.fold_in(key, 99), 3)
    col_pos = jnp.arange(D, dtype=jnp.float32) / D
    col_scale = jnp.exp(jnp.log(10.0) * col_pos) * jax.random.uniform(key_cols, (D,), jnp.float32, 0.5, 1.5)
    row_scale = jnp.exp(jnp.log(10.0) * jax.random.uniform(key_rows, (IMAGES, SEQ, 1), jnp.float32))
    values = jnp.clip(jax.random.normal(key_base, (IMAGES, SEQ, D), jnp.float32), -4.0, 4.0)
    return values * col_scale * row_scale / 8.0


def raised(drawn, key, source, target, shards_of, factor):
    owner, partner = [(jnp.arange(drawn.shape[axis_at]) // (drawn.shape[axis_at] // shards_of)).reshape([-1 if axis == axis_at else 1 for axis in range(drawn.ndim)]) for axis_at in (source, target)]
    chosen = jax.random.permutation(key, shards_of)[partner]
    strong = (owner == chosen) | (owner == (partner + shards_of // 2) % shards_of)
    return jnp.where(strong, factor * drawn, drawn)


def shard_levels(stream_key, shape, pieces, least, largest):
    factor_of, own = 1.0, jax.random.fold_in(stream_key, 6)
    for axis_at, shards_of in pieces:
        steps = jnp.exp(jax.random.uniform(jax.random.fold_in(own, axis_at), (shards_of,), jnp.float32, least / len(pieces), largest / len(pieces)))
        factor_of = factor_of * jnp.repeat(steps, shape[axis_at] // shards_of).reshape([-1 if axis == axis_at else 1 for axis in range(len(shape))])
    return factor_of


def scatter_about(own_key, shape, scale, most, cuts=(), kind=jnp.bfloat16):
    loudness = shard_levels(own_key, shape, cuts, -0.22, 0.18) if cuts else 1.0
    values = jax.random.normal(own_key, shape, jnp.float32) * scale * loudness
    return jnp.minimum(jnp.maximum(values, -most), most).astype(kind)


def gaussian_with(stream_key, extent, deviation, reach, shards, heavy, kind=jnp.bfloat16):
    drawn = deviation * jax.random.normal(stream_key, extent, jnp.float32)
    if shards:
        drawn = drawn * shard_levels(stream_key, extent, shards, -0.22, 0.18)
    return jnp.clip(raised(drawn, jax.random.fold_in(stream_key, 3), *heavy), -reach, reach).astype(kind)


def setup_inputs(seed: int = 0) -> dict:
    key_of = jax.random.split(jax.random.key(seed), 11)
    context = scatter_about(key_of[0], (IMAGES, SEQ, D), 1.0, 6.0, ((0, 4), (1, 2), (2, 4)))
    out_proj = gaussian_with(key_of[1], (D, D), D ** -0.5, 0.125, ((0, 4), (1, 4)), (0, 1, 4, 2.0))
    stream = draw_stream(jax.random.fold_in(key_of[10], 71), 0)
    norm_gain = jnp.clip(1.0 + 0.18 * jax.random.normal(key_of[3], (D,), jnp.float32), 0.1, 1.9)
    expert_ids = draw_expert_ids(jax.random.fold_in(key_of[10], 71), 0)
    slot_ids = draw_slot_ids(jax.random.fold_in(key_of[10], 71), 0)
    gate_probs = jnp.clip(0.02 + 0.28 * jax.random.uniform(key_of[6], (IMAGES, SEQ, TOP), jnp.float32) ** shard_levels(key_of[6], (IMAGES, SEQ, TOP), ((0, 4), (1, 2)), -0.2, 0.2), 0.02, 0.3)
    w_gate = scatter_about(key_of[7], (EXPERTS, HID, D), D ** -0.5, 0.09375, ((0, 8), (1, 4)))
    w_up = scatter_about(key_of[8], (EXPERTS, HID, D), D ** -0.5, 0.09375, ((0, 8), (1, 4)))
    w_down = gaussian_with(key_of[9], (EXPERTS, HID, D), HID ** -0.5, 0.15625, ((0, 8), (1, 4)), (1, 2, 4, 2.0))
    return {"context": context, "out_proj": out_proj, "stream": stream, "norm_gain": norm_gain, "expert_ids": expert_ids, "slot_ids": slot_ids, "gate_probs": gate_probs, "w_gate": w_gate, "w_up": w_up, "w_down": w_down}


eps_value = 1e-05

def reference(context, out_proj, stream, norm_gain, expert_ids, slot_ids, gate_probs, w_gate, w_up, w_down):
    token_count = IMAGES * SEQ
    block_count = token_count // TOK_DEV
    flat_context = context.reshape(token_count, D)
    resid_mid = stream.reshape(token_count, D) + jnp.dot(flat_context, out_proj, preferred_element_type=jnp.float32)
    mean_sq = lax.optimization_barrier(jnp.mean(resid_mid * resid_mid, axis=1, keepdims=True))
    normed = (resid_mid * lax.rsqrt(mean_sq + eps_value) * norm_gain).astype(jnp.bfloat16)
    choice_ids = expert_ids.reshape(token_count, TOP).astype(jnp.int32)
    choice_slots = slot_ids.reshape(token_count, TOP).astype(jnp.int32)
    weights = gate_probs.reshape(token_count, TOP)
    block_of = (jnp.arange(token_count, dtype=jnp.int32) // TOK_DEV)[:, None]
    spill_slot = EXPERTS * block_count * CAP
    target = jnp.where(choice_slots >= 0, (choice_ids * block_count + block_of) * CAP + choice_slots, spill_slot).astype(jnp.int32)
    buffer_rows = jnp.zeros((spill_slot + 1, D), jnp.bfloat16).at[target.reshape(-1)].set(jnp.repeat(normed, TOP, axis=0))
    dispatched = buffer_rows[:spill_slot].reshape(EXPERTS, block_count * CAP, D)

    def expert_hidden(operands):
        inputs, gate_mat, up_mat = operands
        gate_part = jnp.dot(inputs, gate_mat.T, preferred_element_type=jnp.float32)
        up_part = jnp.dot(inputs, up_mat.T, preferred_element_type=jnp.float32)
        return (jax.nn.silu(gate_part) * up_part).astype(jnp.bfloat16)
    hidden = lax.map(expert_hidden, (dispatched, w_gate, w_up))
    slice_width = HID // N_HEAD

    def add_slice(index, total):
        first = index * slice_width
        hidden_slice = lax.dynamic_slice_in_dim(hidden, first, slice_width, 2).astype(jnp.float32)
        down_slice = lax.dynamic_slice_in_dim(w_down, first, slice_width, 1).astype(jnp.float32)
        part = jnp.einsum('erh,ehd->erd', hidden_slice, down_slice, precision=lax.Precision.HIGHEST).astype(jnp.bfloat16)
        lookup = jnp.concatenate([part.reshape(spill_slot, D), jnp.zeros((1, D), jnp.bfloat16)], axis=0)
        picked = lookup[target]
        return total + lax.optimization_barrier(jnp.sum(picked.astype(jnp.float32) * weights[:, :, None], axis=1))
    expert_mix = lax.fori_loop(0, N_HEAD, add_slice, jnp.zeros((token_count, D), jnp.float32))
    return (resid_mid + expert_mix).reshape(IMAGES, SEQ, D)
```

```python
import functools

import jax
import jax.numpy as jnp
from jax import lax
from jax.experimental import pallas as pl
from jax.experimental.pallas import tpu as pltpu
from jax.sharding import PartitionSpec as P

MESH = pl.DeviceIdType.MESH
LANES = 128
F32 = jnp.float32
BF16 = jnp.bfloat16
eps_value = 1e-05
HALVES = 2


def partner(a, k):
    out, bit = a, 1
    while bit <= k:
        if k & bit:
            out = out + bit - 2 * bit * lax.rem(lax.div(out, bit), 2)
        bit *= 2
    return out


def kernel(
    n_tok, n_head, n_exp,
    ctx_ref, proj_hbm, stream_ref, gain_ref, ids_ref, slots_ref, probs_ref,
    wg_hbm, wu_hbm, wd_hbm,
    out_ref,
    proj, wbuf, ctx_all, wall, stream_bf, stream_t, pbf, pown, prs,
    attn_buf, attn_in, ssq, x, gacc, uacc, hid, acc, own, obf, tin, hsend, hrecv, zsend, zrecv,
    proj_sem, w_sem, l_sem, d_sem, ctx_s, ctx_r, wz_s, wz_r, wt_s, wt_r, st_s, st_r,
    prs_s, prs_r, at_s, at_r, xz_s, xz_r, qz_s, qz_r, xh_s, xh_r, qh_s, qh_r,
    xt_s, xt_r, qt_s, qt_r, to_s, to_r, ho_s, ho_r, zo_s, zo_r,
):
    t, h, e = lax.axis_index("tok"), lax.axis_index("head"), lax.axis_index("exp")
    rows, width = stream_ref.shape
    n_local, n_hid, model = wg_hbm.shape
    depth = ctx_ref.shape[1]
    tokens = n_tok * n_exp * rows
    half = width // HALVES
    turned = {"tok": t, "head": e, "exp": h}
    mine = h == e

    def send(src, dst, s_sem, r_sem, device):
        return pltpu.make_async_remote_copy(
            src_ref=src, dst_ref=dst, send_sem=s_sem, recv_sem=r_sem,
            device_id=device, device_id_type=MESH,
        )

    exp_of = [partner(e, k) for k in range(n_exp)]
    head_of = [partner(h, k) for k in range(n_head)]
    on_exp = [{"exp": i} for i in exp_of]
    on_head = [{"head": i} for i in head_of]
    on_tok = {"tok": 1 - t}

    def lanes(i, size):
        return pl.ds(pl.multiple_of(i * size, min(size, LANES)), size)

    n_part = max(1, n_local - 1)
    n_steps = n_head * HALVES
    proj_c = pltpu.make_async_copy(proj_hbm, proj, proj_sem)
    proj_c.start()

    def w_copy(q):
        source = (wg_hbm, wu_hbm)[q % 2].at[q // 2]
        return pltpu.make_async_copy(source, wbuf.at[q], w_sem.at[q])

    free = [(q, i * width, -1) for q in range(2 * n_part, wbuf.shape[0]) for i in range(n_exp)]
    free += [(q, exp_of[p] * width, p) for p in range(n_exp) for q in range(2 * n_part)]

    def unit(n, size):
        per = width // size
        slot, at, p = free[n // per]
        return slot, pl.ds(pl.multiple_of(at + n % per * size, LANES), size), p

    n_late = (n_local - n_part) * 2 * n_exp

    def late(j, m, i):
        return unit(((j - n_part) * 2 + m) * n_exp + i, width)

    def late_copy(j, m, i):
        slot, cols, _ = late(j, m, i)
        source = (wg_hbm, wu_hbm)[m].at[j, :, pl.ds(i * width, width)]
        return pltpu.make_async_copy(
            source, wbuf.at[slot, :, cols], l_sem.at[((j - n_part) * 2 + m) * n_exp + i]
        )

    steps = [(k, c) for c in range(HALVES) for k in range(n_head - 1, -1, -1)]

    def down(s, j):
        return unit(n_late * HALVES + s * n_local + j, half)

    def d_copy(s, j):
        k, c = steps[s]
        slot, cols, _ = down(s, j)
        return pltpu.make_async_copy(
            wd_hbm.at[j, :, lanes(head_of[k] * HALVES + c, half)],
            wbuf.at[slot, :, cols],
            d_sem.at[s, j],
        )

    def load_after(p):
        for j in range(n_part, n_local):
            for m in range(2):
                for i in range(n_exp):
                    if late(j, m, i)[2] == p:
                        late_copy(j, m, i).start()
        for s in range(n_steps):
            for j in range(n_local):
                if down(s, j)[2] == p:
                    d_copy(s, j).start()

    barrier = pltpu.get_barrier_semaphore()
    for device in on_exp[1:] + on_head[1:] + [on_tok]:
        pl.semaphore_signal(barrier, inc=1, device_id=device, device_id_type=MESH)

    @pl.when(jnp.logical_not(mine))
    def _():
        pl.semaphore_signal(barrier, inc=1, device_id=turned, device_id_type=MESH)

    stream_bf[...] = stream_ref[...].astype(BF16)
    lane = lax.broadcasted_iota(jnp.int32, (rows, LANES), 1)
    n_experts = wall.shape[2]
    expert_row = lax.broadcasted_iota(jnp.int32, (n_experts, rows), 0)
    dense = jnp.zeros((n_experts, rows), F32)
    for k in range(ids_ref.shape[0]):
        hit = (ids_ref[k : k + 1, :] == expert_row) & (slots_ref[k : k + 1, :] >= 0)
        dense = dense + jnp.where(hit, probs_ref[k : k + 1, :], 0.0)
    wall[0, e] = jnp.zeros((n_experts, LANES), F32)
    wall[0, e, :, :rows] = dense

    @pl.when(mine)
    def _():
        pl.semaphore_wait(barrier, n_exp - 1 + n_head - 1 + 1)

    @pl.when(jnp.logical_not(mine))
    def _():
        pl.semaphore_wait(barrier, n_exp - 1 + n_head - 1 + 2)

    order = list(range(n_exp - 1, 0, -1))
    ctx_c = {
        k: send(ctx_ref, ctx_all.at[e], ctx_s.at[k], ctx_r.at[k], on_exp[k]) for k in order
    }
    for k in order:
        ctx_c[k].start()
    stream_c = send(stream_bf, stream_t, st_s, st_r, turned)
    wz_c = [
        send(wall.at[0, e], wall.at[0, e], wz_s.at[k], wz_r.at[k], on_exp[k])
        for k in range(1, n_exp)
    ]
    proj_c.wait()
    for q in range(2 * n_part):
        w_copy(q).start()
    load_after(-1)

    def prs_c(j):
        i = exp_of[j]
        return send(pbf.at[i], prs.at[h], prs_s.at[j], prs_r.at[h], {"head": i})

    tile = min(width, 256)
    for j in [0] + order:
        image = exp_of[j]
        if j:
            ctx_c[j].wait_recv()
        source = ctx_all.at[image] if j else ctx_ref

        def project(i, carry):
            cols = lanes(i, tile)
            part = jnp.dot(source[...], proj[:, cols], preferred_element_type=F32)
            pbf[image, :, cols] = part.astype(BF16)

            @pl.when(image == h)
            def _():
                pown[:, cols] = part

            return carry

        lax.fori_loop(0, width // tile, project, 0)

        @pl.when(image != h)
        def _():
            prs_c(j).start()

        if j == order[0]:

            @pl.when(jnp.logical_not(mine))
            def _():
                stream_c.start()

    for k in range(1, n_head):
        source = head_of[k]
        send(pbf.at[0], prs.at[source], prs_s.at[0], prs_r.at[source], on_head[k]).wait_recv()
    attn = pown[...]
    for k in range(1, n_head):
        attn = attn + prs[head_of[k]].astype(F32)
    attn_buf[...] = attn

    @pl.when(jnp.logical_not(mine))
    def _():
        stream_c.wait()

    @pl.when(mine)
    def _():
        stream_t[...] = stream_bf[...]

    attn_c = send(attn_buf, attn_in, at_s, at_r, turned)

    own_cols = lanes(e, width)
    resid = attn + stream_t[...].astype(F32)
    x[0, h, :, own_cols] = (resid * gain_ref[:, own_cols]).astype(BF16)
    square = jnp.sum(resid * resid, axis=1, keepdims=True)
    row_id = lax.broadcasted_iota(jnp.int32, (rows, LANES), 0)
    flat = jnp.sum(jnp.where(row_id == lane, square, 0.0), axis=0, keepdims=True)
    ssq[0, h, e] = jnp.broadcast_to(flat, (8, LANES))

    def x_at(s, k, j):
        return x.at[s, head_of[k], :, lanes(exp_of[j], width)]

    xz_c = {
        j: send(x_at(0, 0, 0), x_at(0, 0, 0), xz_s.at[j], xz_r.at[j], on_exp[j])
        for j in range(1, n_exp)
    }
    xh_c = {
        (k, j): send(x_at(0, 0, j), x_at(0, 0, j), xh_s.at[k, j], xh_r.at[k, j], on_head[k])
        for k in range(1, n_head) for j in range(n_exp)
    }
    xt_c = {
        (k, j): send(x_at(0, k, j), x_at(1, k, j), xt_s.at[k, j], xt_r.at[k, j], on_tok)
        for k in range(n_head) for j in range(n_exp)
    }
    qz_c = [
        send(ssq.at[0, h, e], ssq.at[0, h, e], qz_s.at[k], qz_r.at[k], on_exp[k])
        for k in range(1, n_exp)
    ]
    qh_c = [
        send(ssq.at[0, h], ssq.at[0, h], qh_s.at[k], qh_r.at[k], on_head[k])
        for k in range(1, n_head)
    ]
    qt_c = send(ssq.at[0], ssq.at[1], qt_s, qt_r, on_tok)
    wt_c = send(wall.at[0], wall.at[1], wt_s, wt_r, on_tok)

    def forward(j):
        if j >= n_exp:
            return
        if j:
            xz_c[j].wait_recv()
        for k in range(1, n_head):
            xh_c[k, j].start()
        xt_c[0, j].start()

    def share(j):
        if j >= n_exp:
            return
        for k in range(1, n_head):
            xh_c[k, j].wait_recv()
            xt_c[k, j].start()

    def small(p):
        if p == 0:
            for c in qz_c:
                c.wait_recv()
            for c in qh_c + wz_c:
                c.start()
        if p == max(1, n_exp - 2):
            for c in qh_c:
                c.wait_recv()
            qt_c.start()
            for c in wz_c:
                c.wait()
            wt_c.start()

            @pl.when(jnp.logical_not(mine))
            def _():
                attn_c.start()

    forward(0)
    for j in range(1, n_exp):
        xz_c[j].start()
    for c in qz_c:
        c.start()
    forward(1)
    share(0)
    forward(2)

    token_row = lax.rem(lax.broadcasted_iota(jnp.int32, (tokens, LANES), 0), rows)
    token_lane = lax.broadcasted_iota(jnp.int32, (tokens, LANES), 1)

    def column(value):
        wide = jnp.broadcast_to(value, (n_tok, n_exp, rows, LANES)).reshape(tokens, LANES)
        return jnp.sum(jnp.where(token_row == token_lane, wide, 0.0), axis=1, keepdims=True)

    hid_tile = 256 if n_hid % 256 == 0 else n_hid
    n_tiles = n_hid // hid_tile
    dims = (((1,), (1,)), ((), ()))

    def factors(j):
        sums = column(jnp.sum(ssq[...], axis=2)[:, :, 0:1, :])
        scale = lax.rsqrt(sums / model + eps_value)
        number = (t * n_exp + e) * n_local + j
        expert_of = lax.broadcasted_iota(jnp.int32, wall.shape, 2)
        picked = jnp.where(expert_of == number, wall[...], 0.0)
        return scale, column(jnp.sum(picked, axis=2, keepdims=True))

    def finish(q, g, u, scale, gate_w):
        g = g * scale
        u = u * scale
        hid[q] = (g / (1.0 + jnp.exp(-g)) * u * gate_w).astype(BF16)

    def up_part(j, p):
        cols = lanes(exp_of[p], width)
        scale, gate_w = factors(j) if p == n_exp - 1 else (None, None)

        def body(i, carry):
            q = j * n_tiles + i
            span = lanes(i, hid_tile)
            xv = x[:, :, :, cols].reshape(tokens, width)
            g = lax.dot_general(xv, wbuf[2 * j, span, cols], dims, preferred_element_type=F32)
            u = lax.dot_general(xv, wbuf[2 * j + 1, span, cols], dims, preferred_element_type=F32)
            if p:
                g = g + gacc[q]
                u = u + uacc[q]
            if p < n_exp - 1:
                gacc[q] = g
                uacc[q] = u
            else:
                finish(q, g, u, scale, gate_w)
            return carry

        lax.fori_loop(0, n_tiles, body, 0, unroll=True)

    def up_whole(j):
        scale, gate_w = factors(j)

        def body(i, carry):
            span = lanes(i, hid_tile)
            both = []
            for m in range(2):
                value = jnp.zeros((tokens, hid_tile), F32)
                for n in range(n_exp):
                    slot, cols, _ = late(j, m, n)
                    value = value + lax.dot_general(
                        x[:, :, :, n * width : (n + 1) * width].reshape(tokens, width),
                        wbuf[slot, span, cols], dims, preferred_element_type=F32,
                    )
                both.append(value)
            finish(j * n_tiles + i, both[0], both[1], scale, gate_w)
            return carry

        lax.fori_loop(0, n_tiles, body, 0, unroll=True)

    for p in range(n_exp):
        for k in range(n_head):
            xt_c[k, p].wait_recv()
        if p == n_exp - 1:
            qt_c.wait_recv()
            wt_c.wait()
        for j in range(n_part):
            if p == 0:
                w_copy(2 * j).wait()
                w_copy(2 * j + 1).wait()
            up_part(j, p)
            if j == 0:
                forward(p + 3)
                small(p)
            if j == max(0, n_part - 2):
                share(p + 1)
        load_after(p)
    for j in range(n_part, n_local):
        for m in range(2):
            for i in range(n_exp):
                late_copy(j, m, i).wait()
        up_whole(j)

    to_c = [send(obf.at[s], tin.at[s], to_s.at[s], to_r.at[s], on_tok) for s in range(n_steps)]
    group = n_exp // 2
    near = lax.div(e, group) * group
    first_of = (near, (n_exp - group) - near)

    def ho_c(k, c, g):
        at = (c, k - 1, pl.ds(first_of[g], group))
        return send(hsend.at[at], hrecv.at[at], ho_s.at[k, c, g], ho_r.at[k, c, g], on_head[k])

    def zo_c(m, c):
        at = (c, m - 1)
        return send(zsend.at[at], zrecv.at[at], zo_s.at[m, c], zo_r.at[m, c], on_exp[m])

    def head_step(s):
        k, c = steps[s]
        to_c[s].wait_recv()
        if k:
            hsend[c, k - 1] = (acc[s % 2] + tin[s].astype(F32)).astype(BF16)
            for g in (1, 0):
                ho_c(k, c, g).start()
        else:
            own[c] = acc[s % 2] + tin[s].astype(F32)

    def summed(m, c):
        value = own[c, exp_of[m]]
        for k in range(1, n_head):
            value = value + hrecv[c, k - 1, exp_of[m]].astype(F32)
        return value

    def exp_step(c):
        for m in range(n_exp - 1, 0, -1):
            if m in (n_exp - 1, group - 1):
                for k in range(1, n_head):
                    ho_c(k, c, m // group).wait_recv()
            zsend[c, m - 1] = summed(m, c).astype(BF16)
            zo_c(m, c).start()

    for s in range(n_steps):
        for j in range(n_local):
            d_copy(s, j).wait()
        value = jnp.zeros((tokens, half), F32)
        for j in range(n_local):
            slot, cols, _ = down(s, j)
            for i in range(n_tiles):
                value = value + jnp.dot(
                    hid[j * n_tiles + i],
                    wbuf[slot, i * hid_tile : (i + 1) * hid_tile, cols],
                    preferred_element_type=F32,
                )
        value = value.reshape(n_tok, n_exp, rows, half)
        acc[s % 2] = value[0]
        obf[s] = value[1].astype(BF16)
        to_c[s].start()
        if s:
            head_step(s - 1)
    head_step(n_steps - 1)
    for c in list(ctx_c.values()) + list(xz_c.values()) + qz_c + list(xh_c.values()) + qh_c:
        c.wait_send()
    for c in list(xt_c.values()) + [qt_c] + to_c:
        c.wait_send()
    for j in range(n_exp):

        @pl.when(exp_of[j] != h)
        def _():
            prs_c(j).wait_send()

    for c in range(HALVES):
        exp_step(c)

    @pl.when(jnp.logical_not(mine))
    def _():
        attn_c.wait()

    @pl.when(mine)
    def _():
        attn_in[...] = attn_buf[...]

    for c in range(HALVES):
        if group == 1:
            for k in range(1, n_head):
                ho_c(k, c, 0).wait_recv()
        value = summed(0, c) + attn_in[:, c * half : (c + 1) * half]
        for m in range(n_exp - 1, 0, -1):
            zo_c(m, c).wait_recv()
            value = value + zrecv[c, m - 1].astype(F32)
        out_ref[:, c * half : (c + 1) * half] = value

    for c in range(HALVES):
        for k in range(1, n_head):
            for g in range(2):
                ho_c(k, c, g).wait_send()
        for m in range(1, n_exp):
            zo_c(m, c).wait_send()


def solution(mesh):
    n_tok, n_head, n_exp = mesh.shape["tok"], mesh.shape["head"], mesh.shape["exp"]

    def on_device(
        context, out_proj, stream, norm_gain, expert_ids, slot_ids, gate_probs, w_gate, w_up, w_down
    ):
        rows, width = stream.shape[1:]
        n_local, n_hid, model = w_gate.shape
        tokens = n_tok * n_exp * rows
        depth = context.shape[2]
        half = width // HALVES
        n_steps = n_head * HALVES
        hid_tile = 256 if n_hid % 256 == 0 else n_hid
        n_tiles = n_hid // hid_tile
        n_part = max(1, n_local - 1)
        vmem = pl.BlockSpec(memory_space=pltpu.VMEM)
        hbm = pl.BlockSpec(memory_space=pl.ANY)
        dma = pltpu.SemaphoreType.DMA
        V = pltpu.VMEM
        n_slots = max(2 * n_part, 3 * n_local - 2 * n_part)
        n_late = (n_local - n_part) * 2 * n_exp
        scratch = [
            V(out_proj.shape, BF16),
            V((n_slots, n_hid, model), BF16),
            V((n_exp, rows, depth), BF16),
            V((n_tok, n_exp, n_tok * n_exp * n_local, LANES), F32),
            V((rows, width), BF16),
            V((rows, width), BF16),
            V((n_exp, rows, width), BF16),
            V((rows, width), F32),
            V((n_head, rows, width), BF16),
            V((rows, width), F32),
            V((rows, width), F32),
            V((n_tok, n_exp, n_exp, 8, LANES), F32),
            V((n_tok, n_exp, rows, model), BF16),
            V((n_part * n_tiles, tokens, hid_tile), F32),
            V((n_part * n_tiles, tokens, hid_tile), F32),
            V((n_local * n_tiles, tokens, hid_tile), BF16),
            V((2, n_exp, rows, half), F32),
            V((HALVES, n_exp, rows, half), F32),
            V((n_steps, n_exp, rows, half), BF16),
            V((n_steps, n_exp, rows, half), BF16),
            V((HALVES, n_head - 1, n_exp, rows, half), BF16),
            V((HALVES, n_head - 1, n_exp, rows, half), BF16),
            V((HALVES, n_exp - 1, rows, half), BF16),
            V((HALVES, n_exp - 1, rows, half), BF16),
            dma, dma((2 * n_part,)), dma((max(1, n_late),)), dma((n_steps, n_local)),
            dma((n_exp,)), dma((n_exp,)), dma((n_exp,)), dma((n_exp,)), dma, dma, dma, dma,
            dma((n_exp,)), dma((n_head,)), dma, dma,
            dma((n_exp,)), dma((n_exp,)), dma((n_exp,)), dma((n_exp,)),
            dma((n_head, n_exp)), dma((n_head, n_exp)), dma((n_head,)), dma((n_head,)),
            dma((n_head, n_exp)), dma((n_head, n_exp)), dma, dma,
            dma((n_steps,)), dma((n_steps,)),
            dma((n_head, HALVES, 2)), dma((n_head, HALVES, 2)),
            dma((n_exp, HALVES)), dma((n_exp, HALVES)),
        ]
        out = pl.pallas_call(
            functools.partial(kernel, n_tok, n_head, n_exp),
            out_shape=jax.ShapeDtypeStruct((rows, width), F32),
            in_specs=[vmem, hbm, vmem, vmem, vmem, vmem, vmem, hbm, hbm, hbm],
            out_specs=vmem,
            scratch_shapes=scratch,
            compiler_params=pltpu.CompilerParams(
                collective_id=0, has_side_effects=True, vmem_limit_bytes=67_043_328
            ),
        )(
            context[0], out_proj, stream[0], norm_gain[None], expert_ids[0].T, slot_ids[0].T,
            gate_probs[0].T, w_gate, w_up, w_down,
        )
        return stream + out[None]

    in_specs = (
        P("exp", "tok", "head"),
        P("head", "exp"),
        P("exp", "tok", "head"),
        P(),
        P("exp", "tok", None),
        P("exp", "tok", None),
        P("exp", "tok", None),
        P(("tok", "exp"), "head", None),
        P(("tok", "exp"), "head", None),
        P(("tok", "exp"), "head", None),
    )
    return jax.shard_map(
        on_device, mesh=mesh, in_specs=in_specs, out_specs=P("exp", "tok", "head"), check_vma=False
    )
```

```python
import functools

import jax
import jax.numpy as jnp
from jax import lax
from jax.experimental import pallas as pl
from jax.experimental.pallas import tpu as pltpu
from jax.sharding import PartitionSpec as P

MESH = pl.DeviceIdType.MESH
LANES = 128
F32 = jnp.float32
BF16 = jnp.bfloat16
eps_value = 1e-05
VMEM_BYTES = 62_500_000


def parts_of(width):
    sizes = (width // 2, width // 4, width // 4) if width % 512 == 0 else (width // 2, width // 2)
    return [(sum(sizes[:i]), size) for i, size in enumerate(sizes)]


def steps_of(width, n_head):
    far, middle = n_head - 1, n_head // 2
    first = [k for k in range(far - 1, 0, -1)] + [far, 0]
    rest = [middle] + [k for k in range(far, 0, -1) if k != middle] + [0]
    return [(k, c) for c in range(len(parts_of(width))) for k in (rest if c else first)]


def partner(a, k):
    out, bit = a, 1
    while bit <= k:
        if k & bit:
            out = out + bit - 2 * bit * lax.rem(lax.div(out, bit), 2)
        bit *= 2
    return out


def kernel(
    n_tok, n_head, n_exp,
    ctx_ref, proj_hbm, stream_ref, gain_ref, ids_ref, slots_ref, probs_ref,
    wg_hbm, wu_hbm, wd_hbm,
    out_ref,
    proj, wbuf, ctx_all, wall, stream_bf, stream_t, pbf, pown, prs,
    attn_buf, attn_in, ssq, x, gacc, uacc, hid, acc, own, obf, tin, hsend, hrecv, zsend, zrecv,
    fown, fzsend, fzrecv, fsend, frecv,
    proj_sem, w_sem, l_sem, d_sem, ctx_s, ctx_r, wz_s, wz_r, wt_s, wt_r, st_s, st_r,
    prs_s, prs_r, at_s, at_r, xz_s, xz_r, qz_s, qz_r, xh_s, xh_r, qh_s, qh_r,
    xt_s, xt_r, qt_s, qt_r, to_s, to_r, ho_s, ho_r, zo_s, zo_r, fz_s, fz_r, fh_s, fh_r,
):
    t, h, e = lax.axis_index("tok"), lax.axis_index("head"), lax.axis_index("exp")
    rows, width = stream_ref.shape
    n_local, n_hid, model = wg_hbm.shape
    depth = ctx_ref.shape[1]
    tokens = n_tok * n_exp * rows
    parts = parts_of(width)
    turned = {"tok": t, "head": e, "exp": h}
    mine = h == e

    def send(src, dst, s_sem, r_sem, device):
        return pltpu.make_async_remote_copy(
            src_ref=src, dst_ref=dst, send_sem=s_sem, recv_sem=r_sem,
            device_id=device, device_id_type=MESH,
        )

    def sent(ref, sem):
        send(ref, ref, sem, sem, {"tok": 1 - t}).wait_send()

    def arrived(ref, sem):
        send(ref, ref, sem, sem, {"tok": 1 - t}).wait_recv()

    def loaded(ref, sem):
        pltpu.make_async_copy(ref, ref, sem).wait()

    exp_of = [partner(e, k) for k in range(n_exp)]
    head_of = [partner(h, k) for k in range(n_head)]
    on_exp = [{"exp": i} for i in exp_of]
    on_head = [{"head": i} for i in head_of]
    on_tok = {"tok": 1 - t}

    def lanes(i, size):
        return pl.ds(pl.multiple_of(i * size, min(size, LANES)), size)

    n_part = max(1, n_local - 1)
    steps = steps_of(width, n_head)
    n_steps = len(steps)
    proj_c = pltpu.make_async_copy(proj_hbm, proj, proj_sem)
    proj_c.start()

    def w_copy(q):
        source = (wg_hbm, wu_hbm)[q % 2].at[q // 2]
        return pltpu.make_async_copy(source, wbuf.at[q], w_sem.at[q // 2])

    free = [(q, i * width, -1) for q in range(2 * n_part, wbuf.shape[0]) for i in range(n_exp)]
    free += [(q, exp_of[p] * width, p) for p in range(n_exp) for q in range(2 * n_part)]

    def place(at, size):
        slot, first, p = free[at // width]
        return slot, pl.ds(pl.multiple_of(first + at % width, LANES), size), p

    n_late = (n_local - n_part) * 2 * n_exp

    def late(j, m, i):
        return place((((j - n_part) * 2 + m) * n_exp + i) * width, width)

    def late_copy(j, m, i):
        slot, cols, _ = late(j, m, i)
        source = (wg_hbm, wu_hbm)[m].at[j, :, pl.ds(i * width, width)]
        return pltpu.make_async_copy(
            source, wbuf.at[slot, :, cols], l_sem.at[j - n_part]
        )

    down_at, at = {}, n_late * width
    for n, (_, c) in enumerate(steps):
        for j in range(n_local):
            down_at[n, j] = at
            at += parts[c][1]

    def down(s, j):
        return place(down_at[s, j], parts[steps[s][1]][1])

    def d_copy(s, j):
        k, c = steps[s]
        slot, cols, _ = down(s, j)
        first, size = parts[c]
        source = wd_hbm.at[j, :, pl.ds(pl.multiple_of(head_of[k] * width + first, LANES), size)]
        return pltpu.make_async_copy(source, wbuf.at[slot, :, cols], d_sem.at[s])

    def load_after(p):
        for j in range(n_part, n_local):
            for m in range(2):
                for i in range(n_exp):
                    if late(j, m, i)[2] == p:
                        late_copy(j, m, i).start()
        for s in range(n_steps):
            for j in range(n_local):
                if down(s, j)[2] == p:
                    d_copy(s, j).start()

    barrier = pltpu.get_barrier_semaphore()
    for device in on_exp[1:] + on_head[1:] + [on_tok]:
        pl.semaphore_signal(barrier, inc=1, device_id=device, device_id_type=MESH)

    @pl.when(jnp.logical_not(mine))
    def _():
        pl.semaphore_signal(barrier, inc=1, device_id=turned, device_id_type=MESH)

    stream_bf[...] = stream_ref[...].astype(BF16)
    lane = lax.broadcasted_iota(jnp.int32, (rows, LANES), 1)
    n_experts = wall.shape[2]
    expert_row = lax.broadcasted_iota(jnp.int32, (n_experts, rows), 0)
    dense = jnp.zeros((n_experts, rows), F32)
    for k in range(ids_ref.shape[0]):
        hit = (ids_ref[k : k + 1, :] == expert_row) & (slots_ref[k : k + 1, :] >= 0)
        dense = dense + jnp.where(hit, probs_ref[k : k + 1, :], 0.0)
    wall[0, e] = jnp.zeros((n_experts, LANES), F32)
    wall[0, e, :, :rows] = dense

    @pl.when(mine)
    def _():
        pl.semaphore_wait(barrier, n_exp - 1 + n_head - 1 + 1)

    @pl.when(jnp.logical_not(mine))
    def _():
        pl.semaphore_wait(barrier, n_exp - 1 + n_head - 1 + 2)

    order = list(range(n_exp - 1, 0, -1))
    ctx_c = {
        k: send(ctx_ref, ctx_all.at[e], ctx_s, ctx_r.at[k], on_exp[k]) for k in order
    }
    for k in order:
        ctx_c[k].start()
    stream_c = send(stream_bf, stream_t, st_s, st_r, turned)
    wz_c = [
        send(wall.at[0, e], wall.at[0, e], wz_s, wz_r, on_exp[k])
        for k in range(1, n_exp)
    ]
    proj_c.wait()
    for q in range(2 * n_part):
        w_copy(q).start()
    load_after(-1)

    def prs_c(j):
        i = exp_of[j]
        return send(pbf.at[i], prs.at[h], prs_s, prs_r, {"head": i})

    tile = min(width, 256)
    for group in [[0]] + [order[:1]] + [order[i : i + 2] for i in range(1, len(order), 2)]:
        pieces = []
        for j in group:
            if j:
                ctx_c[j].wait_recv()
            pieces.append(ctx_all[exp_of[j]] if j else ctx_ref[...])
        pieces = jnp.concatenate(pieces, axis=0)

        def project(i, carry):
            cols = lanes(i, tile)
            part = jnp.dot(pieces, proj[:, cols], preferred_element_type=F32)
            for n, j in enumerate(group):
                mine_part = part[n * rows : (n + 1) * rows]
                pbf[exp_of[j], :, cols] = mine_part.astype(BF16)

                @pl.when(exp_of[j] == h)
                def _():
                    pown[:, cols] = mine_part

            return carry

        lax.fori_loop(0, width // tile, project, 0, unroll=True)
        for j in group:

            @pl.when(exp_of[j] != h)
            def _():
                prs_c(j).start()

        if group == order[:1]:

            @pl.when(jnp.logical_not(mine))
            def _():
                stream_c.start()

    arrived(prs.at[pl.ds(0, n_head - 1)], prs_r)
    attn = pown[...]
    for k in range(1, n_head):
        attn = attn + prs[head_of[k]].astype(F32)
    attn_buf[...] = attn

    @pl.when(jnp.logical_not(mine))
    def _():
        stream_c.wait()

    @pl.when(mine)
    def _():
        stream_t[...] = stream_bf[...]

    attn_c = send(attn_buf, attn_in, at_s, at_r, turned)

    own_cols = lanes(e, width)
    resid = attn + stream_t[...].astype(F32)
    x[0, h, :, own_cols] = (resid * gain_ref[:, own_cols]).astype(BF16)
    square = jnp.sum(resid * resid, axis=1, keepdims=True)
    row_id = lax.broadcasted_iota(jnp.int32, (rows, LANES), 0)
    flat = jnp.sum(jnp.where(row_id == lane, square, 0.0), axis=0, keepdims=True)
    ssq[0, h, e] = jnp.broadcast_to(flat, (8, LANES))

    def x_at(s, k, j):
        return x.at[s, head_of[k], :, lanes(exp_of[j], width)]

    xz_c = {
        j: send(x_at(0, 0, 0), x_at(0, 0, 0), xz_s, xz_r.at[j], on_exp[j])
        for j in range(1, n_exp)
    }
    xh_c = {
        (k, j): send(x_at(0, 0, j), x_at(0, 0, j), xh_s, xh_r.at[k - 1, j], on_head[k])
        for k in range(1, n_head) for j in range(n_exp)
    }
    xt_c = {
        (k, j): send(x_at(0, k, j), x_at(1, k, j), xt_s, xt_r.at[j], on_tok)
        for k in range(n_head) for j in range(n_exp)
    }
    qz_c = [
        send(ssq.at[0, h, e], ssq.at[0, h, e], qz_s, qz_r, on_exp[k])
        for k in range(1, n_exp)
    ]
    qh_c = [
        send(ssq.at[0, h], ssq.at[0, h], qh_s, qh_r, on_head[k])
        for k in range(1, n_head)
    ]
    qt_c = send(ssq.at[0], ssq.at[1], qt_s, qt_r, on_tok)
    wt_c = send(wall.at[0], wall.at[1], wt_s, wt_r, on_tok)

    def forward(j):
        if j >= n_exp:
            return
        if j:
            xz_c[j].wait_recv()
        for k in range(1, n_head):
            xh_c[k, j].start()
        xt_c[0, j].start()

    def share(j):
        if j >= n_exp:
            return
        for k in range(1, n_head):
            xh_c[k, j].wait_recv()
            xt_c[k, j].start()

    def small(p):
        if p == 0:
            arrived(ssq.at[0, 0, pl.ds(0, n_exp - 1)], qz_r)
            for c in qh_c + wz_c:
                c.start()
        if p == max(1, n_exp - 2):
            arrived(ssq.at[0, pl.ds(0, n_head - 1)], qh_r)
            qt_c.start()
            arrived(wall.at[0, pl.ds(0, n_exp - 1)], wz_r)
            wt_c.start()

            @pl.when(jnp.logical_not(mine))
            def _():
                attn_c.start()

    forward(0)
    for j in range(1, n_exp):
        xz_c[j].start()
    for c in qz_c:
        c.start()
    forward(1)
    share(0)
    forward(2)

    token_row = lax.rem(lax.broadcasted_iota(jnp.int32, (tokens, LANES), 0), rows)
    token_lane = lax.broadcasted_iota(jnp.int32, (tokens, LANES), 1)

    def column(value):
        wide = jnp.broadcast_to(value, (n_tok, n_exp, rows, LANES)).reshape(tokens, LANES)
        return jnp.sum(jnp.where(token_row == token_lane, wide, 0.0), axis=1, keepdims=True)

    hid_tile = 256 if n_hid % 256 == 0 else n_hid
    n_tiles = n_hid // hid_tile
    dims = (((1,), (1,)), ((), ()))

    def factors(j):
        sums = column(jnp.sum(ssq[...], axis=2)[:, :, 0:1, :])
        scale = lax.rsqrt(sums / model + eps_value)
        number = (t * n_exp + e) * n_local + j
        expert_of = lax.broadcasted_iota(jnp.int32, wall.shape, 2)
        picked = jnp.where(expert_of == number, wall[...], 0.0)
        return scale, column(jnp.sum(picked, axis=2, keepdims=True))

    def finish(j, i, g, u, scale, gate_w):
        g = g * scale
        u = u * scale
        hid[j, :, lanes(i, hid_tile)] = (g / (1.0 + jnp.exp(-g)) * u * gate_w).astype(BF16)

    def up_part(j, p):
        cols = lanes(exp_of[p], width)
        scale, gate_w = factors(j) if p == n_exp - 1 else (None, None)

        def body(i, carry):
            q = j * n_tiles + i
            span = lanes(i, hid_tile)
            xv = x[:, :, :, cols].reshape(tokens, width)
            g = lax.dot_general(xv, wbuf[2 * j, span, cols], dims, preferred_element_type=F32)
            u = lax.dot_general(xv, wbuf[2 * j + 1, span, cols], dims, preferred_element_type=F32)
            if p:
                g = g + gacc[q]
                u = u + uacc[q]
            if p < n_exp - 1:
                gacc[q] = g
                uacc[q] = u
            else:
                finish(j, i, g, u, scale, gate_w)
            return carry

        lax.fori_loop(0, n_tiles, body, 0, unroll=True)

    def up_whole(j):
        scale, gate_w = factors(j)

        def body(i, carry):
            span = lanes(i, hid_tile)
            both = []
            for m in range(2):
                value = jnp.zeros((tokens, hid_tile), F32)
                for n in range(n_exp):
                    slot, cols, _ = late(j, m, n)
                    value = value + lax.dot_general(
                        x[:, :, :, n * width : (n + 1) * width].reshape(tokens, width),
                        wbuf[slot, span, cols], dims, preferred_element_type=F32,
                    )
                both.append(value)
            finish(j, i, both[0], both[1], scale, gate_w)
            return carry

        lax.fori_loop(0, n_tiles, body, 0, unroll=True)

    for p in range(n_exp):
        arrived(pbf, xt_r.at[p])
        if p == n_exp - 1:
            qt_c.wait_recv()
            wt_c.wait_recv()
        for j in range(n_part):
            if p == 0:
                loaded(wbuf.at[pl.ds(0, 2)], w_sem.at[j])
            up_part(j, p)
            if j == 0:
                forward(p + 3)
                small(p)
            if j == max(0, n_part - 2):
                share(p + 1)
        load_after(p)
    for j in range(n_part, n_local):
        loaded(wbuf.at[pl.ds(0, 2)], l_sem.at[j - n_part])
        up_whole(j)

    far = n_head - 1
    to_c = [
        send(obf[c].at[k], tin[c].at[k], to_s.at[c], to_r.at[k, c], on_tok) for k, c in steps
    ]
    group = n_exp // 2
    near = lax.div(e, group) * group
    first_of = (near, (n_exp - group) - near)

    def heads_of(c):
        return range(1, n_head) if c else range(1, far)

    def ho_c(k, c, g):
        at = (k - 1, pl.ds(first_of[g], group))
        return send(
            hsend[c].at[at], hrecv[c].at[at], ho_s.at[c], ho_r.at[c, g], on_head[k]
        )

    def zo_c(m, c):
        return send(zsend[c].at[m - 1], zrecv[c].at[m - 1], zo_s.at[c], zo_r.at[c], on_exp[m])

    def heads_arrived(c, g):
        arrived(hrecv[c].at[pl.ds(0, len(heads_of(c))), pl.ds(0, group)], ho_r.at[c, g])

    fz_c = [
        send(fzsend.at[m - 1], fzrecv.at[m - 1], fz_s, fz_r, on_exp[m])
        for m in range(1, n_exp)
    ]
    fh_c = send(fsend, frecv, fh_s, fh_r, on_head[far])

    def head_step(s):
        k, c = steps[s]
        to_c[s].wait_recv()
        if k == far and c == 0:
            for m in range(n_exp - 1, -1, -1):
                i = exp_of[m]
                value = acc[c][s % 4, i] + tin[c][k, i].astype(F32)
                if m:
                    fzsend[m - 1] = value.astype(BF16)
                    fz_c[m - 1].start()
                else:
                    fown[...] = value
        elif k:
            hsend[c][k - 1] = (acc[c][s % 4] + tin[c][k].astype(F32)).astype(BF16)
            for g in (1, 0):
                ho_c(k, c, g).start()
        else:
            own[c][...] = acc[c][s % 4] + tin[c][k].astype(F32)

    def far_step():
        value = fown[...]
        arrived(fzrecv, fz_r)
        for m in range(n_exp - 1, 0, -1):
            value = value + fzrecv[m - 1].astype(F32)
        fsend[...] = value.astype(BF16)
        fh_c.start()

    def summed(m, c):
        value = own[c][exp_of[m]]
        for k in heads_of(c):
            value = value + hrecv[c][k - 1, exp_of[m]].astype(F32)
        return value

    def exp_step(c):
        for m in range(n_exp - 1, 0, -1):
            if m in (n_exp - 1, group - 1):
                heads_arrived(c, m // group)
            zsend[c][m - 1] = summed(m, c).astype(BF16)
            zo_c(m, c).start()

    def down_steps(batch):
        size = parts[steps[batch[0]][1]][1]
        for s in batch:
            loaded(wbuf.at[0, :, pl.ds(0, n_local * size)], d_sem.at[s])
        values = [jnp.zeros((tokens, size), F32) for _ in batch]
        for j in range(n_local):
            for n, s in enumerate(batch):
                slot, cols, _ = down(s, j)
                values[n] = values[n] + jnp.dot(
                    hid[j], wbuf[slot, :, cols], preferred_element_type=F32
                )
        for s, value in zip(batch, values):
            k, c = steps[s]
            value = value.reshape(n_tok, n_exp, rows, size)
            acc[c][s % 4] = value[0]
            obf[c][k] = value[1].astype(BF16)
            to_c[s].start()

    batches, s = [], 0
    while s < n_steps:
        n = 1 if parts[steps[s][1]][1] > 256 else 2
        batches.append(range(s, s + n))
        s += n
    for b, batch in enumerate(batches):
        down_steps(batch)
        for s in batches[b - 1] if b else ():
            head_step(s)
        if len(parts) > 2 and batch[-1] == 2 * n_head + 1:
            exp_step(0)
    for s in batches[-1]:
        head_step(s)
    some = pl.ds(0, n_exp - 1)
    sent(ctx_all.at[some], ctx_s)
    sent(pbf.at[some], prs_s)
    sent(pbf.at[some], xz_s)
    sent(x.at[0, pl.ds(0, n_head - 1)], xh_s)
    sent(x.at[0], xt_s)
    sent(ssq.at[0, 0, some], qz_s)
    sent(ssq.at[0, pl.ds(0, n_head - 1)], qh_s)
    sent(wall.at[0, some], wz_s)
    wt_c.wait_send()
    qt_c.wait_send()
    far_step()
    for c in range(1 if len(parts) > 2 else 0, len(parts)):
        exp_step(c)

    @pl.when(jnp.logical_not(mine))
    def _():
        attn_c.wait()

    @pl.when(mine)
    def _():
        attn_in[...] = attn_buf[...]

    for c, (first, size) in enumerate(parts):
        if group == 1:
            heads_arrived(c, 0)
        value = summed(0, c) + attn_in[:, first : first + size]
        if c == 0:
            fh_c.wait_recv()
            value = value + frecv[...].astype(F32)
        arrived(zrecv[c], zo_r.at[c])
        for m in range(n_exp - 1, 0, -1):
            value = value + zrecv[c][m - 1].astype(F32)
        out_ref[:, first : first + size] = value

    for c in range(len(parts)):
        sent(obf[c], to_s.at[c])
        sent(hsend[c].at[pl.ds(0, len(heads_of(c)))], ho_s.at[c])
        sent(zsend[c], zo_s.at[c])
    sent(fzsend, fz_s)
    fh_c.wait_send()


def solution(mesh):
    n_tok, n_head, n_exp = mesh.shape["tok"], mesh.shape["head"], mesh.shape["exp"]

    def on_device(
        context, out_proj, stream, norm_gain, expert_ids, slot_ids, gate_probs, w_gate, w_up, w_down
    ):
        rows, width = stream.shape[1:]
        n_local, n_hid, model = w_gate.shape
        tokens = n_tok * n_exp * rows
        depth = context.shape[2]
        parts = parts_of(width)
        n_parts = len(parts)
        n_steps = len(steps_of(width, n_head))
        hid_tile = 256 if n_hid % 256 == 0 else n_hid
        n_tiles = n_hid // hid_tile
        n_part = max(1, n_local - 1)
        vmem = pl.BlockSpec(memory_space=pltpu.VMEM)
        hbm = pl.BlockSpec(memory_space=pl.ANY)
        dma = pltpu.SemaphoreType.DMA
        V = pltpu.VMEM
        n_slots = max(2 * n_part, 3 * n_local - 2 * n_part)
        scratch = [
            V(out_proj.shape, BF16),
            V((n_slots, n_hid, model), BF16),
            V((n_exp, rows, depth), BF16),
            V((n_tok, n_exp, n_tok * n_exp * n_local, LANES), F32),
            V((rows, width), BF16),
            V((rows, width), BF16),
            V((n_exp, rows, width), BF16),
            V((rows, width), F32),
            V((n_head, rows, width), BF16),
            V((rows, width), F32),
            V((rows, width), F32),
            V((n_tok, n_exp, n_exp, 8, LANES), F32),
            V((n_tok, n_exp, rows, model), BF16),
            V((n_part * n_tiles, tokens, hid_tile), F32),
            V((n_part * n_tiles, tokens, hid_tile), F32),
            V((n_local, tokens, n_hid), BF16),
            [V((4, n_exp, rows, size), F32) for _, size in parts],
            [V((n_exp, rows, size), F32) for _, size in parts],
            [V((n_head, n_exp, rows, size), BF16) for _, size in parts],
            [V((n_head, n_exp, rows, size), BF16) for _, size in parts],
            [V((n_head - 1, n_exp, rows, size), BF16) for _, size in parts],
            [V((n_head - 1, n_exp, rows, size), BF16) for _, size in parts],
            [V((n_exp - 1, rows, size), BF16) for _, size in parts],
            [V((n_exp - 1, rows, size), BF16) for _, size in parts],
            V((rows, parts[0][1]), F32),
            V((n_exp - 1, rows, parts[0][1]), BF16),
            V((n_exp - 1, rows, parts[0][1]), BF16),
            V((rows, parts[0][1]), BF16),
            V((rows, parts[0][1]), BF16),
            dma, dma((n_part,)), dma((max(1, n_local - n_part),)), dma((n_steps,)),
            dma, dma((n_exp,)), dma, dma, dma, dma, dma, dma,
            dma, dma, dma, dma,
            dma, dma((n_exp,)), dma, dma, dma, dma((n_head - 1, n_exp)), dma, dma,
            dma, dma((n_exp,)), dma, dma,
            dma((n_parts,)), dma((n_head, n_parts)), dma((n_parts,)), dma((n_parts, 2)),
            dma((n_parts,)), dma((n_parts,)), dma, dma, dma, dma,
        ]
        out = pl.pallas_call(
            functools.partial(kernel, n_tok, n_head, n_exp),
            out_shape=pltpu.VMEM((rows, width), F32),
            in_specs=[vmem, hbm, vmem, vmem, vmem, vmem, vmem, hbm, hbm, hbm],
            out_specs=vmem,
            scratch_shapes=scratch,
            compiler_params=pltpu.CompilerParams(
                collective_id=0, has_side_effects=True, vmem_limit_bytes=VMEM_BYTES
            ),
        )(
            context[0], out_proj, stream[0], norm_gain[None], expert_ids[0].T, slot_ids[0].T,
            gate_probs[0].T, w_gate, w_up, w_down,
        )
        return stream + out[None]

    in_specs = (
        P("exp", "tok", "head"),
        P("head", "exp"),
        P("exp", "tok", "head"),
        P(),
        P("exp", "tok", None),
        P("exp", "tok", None),
        P("exp", "tok", None),
        P(("tok", "exp"), "head", None),
        P(("tok", "exp"), "head", None),
        P(("tok", "exp"), "head", None),
    )
    return jax.shard_map(
        on_device, mesh=mesh, in_specs=in_specs, out_specs=P("exp", "tok", "head"), check_vma=False
    )
```

```python
import functools

import jax
import jax.numpy as jnp
from jax import lax
from jax.experimental import pallas as pl
from jax.experimental.pallas import tpu as pltpu
from jax.sharding import PartitionSpec as P

MESH = pl.DeviceIdType.MESH
LANES = 128
F32 = jnp.float32
BF16 = jnp.bfloat16
eps_value = 1e-05
VMEM_BYTES = 62_500_000


def parts_of(width):
    sizes = (width // 2, width // 4, width // 4) if width % 512 == 0 else (width // 2, width // 2)
    return [(sum(sizes[:i]), size) for i, size in enumerate(sizes)]


def batches_of(width, n_head):
    parts = parts_of(width)
    far, middle = n_head - 1, n_head // 2
    ks = [middle] + [k for k in range(far, 0, -1) if k != middle]
    first = [(k, 0) for k in range(far - 1, 0, -1)] + [(far, 0)]
    rest = [(k, c) for c in range(1, len(parts) - 1) for k in ks]
    rest += [(k, len(parts) - 1) for k in range(far, 0, -1)]
    own = [(0, c) for c in range(1, len(parts))]

    def cut(steps):
        n = 1 if parts[steps[0][1]][1] > 256 else 2
        return [tuple(steps[i : i + n]) for i in range(0, len(steps), n)]

    others = cut(rest)
    return cut(first) + others[:1] + [((0, 0),)] + others[1:] + cut(own)


def partner(a, k):
    out, bit = a, 1
    while bit <= k:
        if k & bit:
            out = out + bit - 2 * bit * lax.rem(lax.div(out, bit), 2)
        bit *= 2
    return out


def kernel(
    n_tok, n_head, n_exp,
    ctx_hbm, proj_hbm, stream_hbm, gain_hbm, ids_hbm, slots_hbm, probs_hbm,
    wg_hbm, wu_hbm, wd_hbm,
    out_ref,
    ctx_ref, stream_ref, gain_ref, ids_ref, slots_ref, probs_ref, in_sem,
    proj, wbuf, ctx_all, wall, stream_bf, stream_t, pbf, pown, prs,
    attn_buf, attn_in, ssq, x, gacc, uacc, hid, acc, own, obf, tin, hsend, hrecv, zsend, zrecv,
    fown, fzsend, fzrecv, fsend, frecv,
    proj_sem, w_sem, l_sem, d_sem, ctx_s, ctx_r, wz_s, wz_r, wt_s, wt_r, st_s, st_r,
    prs_s, prs_r, at_s, at_r, xz_s, xz_r, qz_s, qz_r, xh_s, xh_r, qh_s, qh_r,
    xt_s, xt_r, qt_s, qt_r, to_s, to_r, ho_s, ho_r, zo_s, zo_r, fz_s, fz_r, fh_s, fh_r,
):
    t, h, e = lax.axis_index("tok"), lax.axis_index("head"), lax.axis_index("exp")
    rows, width = stream_ref.shape
    n_local, n_hid, model = wg_hbm.shape
    depth = ctx_ref.shape[1]
    tokens = n_tok * n_exp * rows
    inputs = [
        pltpu.make_async_copy(source, target, in_sem.at[n])
        for n, (source, target) in enumerate((
            (ctx_hbm, ctx_ref), (stream_hbm, stream_ref), (ids_hbm, ids_ref),
            (slots_hbm, slots_ref), (probs_hbm, probs_ref), (gain_hbm, gain_ref),
        ))
    ]
    for c in inputs:
        c.start()
    parts = parts_of(width)
    turned = {"tok": t, "head": e, "exp": h}
    mine = h == e

    def send(src, dst, s_sem, r_sem, device):
        return pltpu.make_async_remote_copy(
            src_ref=src, dst_ref=dst, send_sem=s_sem, recv_sem=r_sem,
            device_id=device, device_id_type=MESH,
        )

    def sent(ref, sem):
        send(ref, ref, sem, sem, {"tok": 1 - t}).wait_send()

    def arrived(ref, sem):
        send(ref, ref, sem, sem, {"tok": 1 - t}).wait_recv()

    def loaded(ref, sem):
        pltpu.make_async_copy(ref, ref, sem).wait()

    exp_of = [partner(e, k) for k in range(n_exp)]
    head_of = [partner(h, k) for k in range(n_head)]
    on_exp = [{"exp": i} for i in exp_of]
    on_head = [{"head": i} for i in head_of]
    on_tok = {"tok": 1 - t}

    barrier = pltpu.get_barrier_semaphore()
    for device in on_exp[1:] + on_head[1:] + [on_tok]:
        pl.semaphore_signal(barrier, inc=1, device_id=device, device_id_type=MESH)

    @pl.when(jnp.logical_not(mine))
    def _():
        pl.semaphore_signal(barrier, inc=1, device_id=turned, device_id_type=MESH)

    def lanes(i, size):
        return pl.ds(pl.multiple_of(i * size, min(size, LANES)), size)

    n_part = max(1, n_local - 1)
    batches = batches_of(width, n_head)
    steps = [step for batch in batches for step in batch]
    proj_c = pltpu.make_async_copy(proj_hbm, proj, proj_sem)
    proj_c.start()

    def w_copy(q):
        source = (wg_hbm, wu_hbm)[q % 2].at[q // 2]
        return pltpu.make_async_copy(source, wbuf.at[q], w_sem.at[q // 2])

    free = [(q, i * width, -1) for q in range(2 * n_part, wbuf.shape[0]) for i in range(n_exp)]
    free += [(q, exp_of[p] * width, p) for p in range(n_exp) for q in range(2 * n_part)]

    def place(at, size):
        slot, first, p = free[at // width]
        return slot, pl.ds(pl.multiple_of(first + at % width, LANES), size), p

    n_late = (n_local - n_part) * 2 * n_exp

    def late(j, m, i):
        return place((((j - n_part) * 2 + m) * n_exp + i) * width, width)

    def late_copy(j, m, i):
        slot, cols, _ = late(j, m, i)
        source = (wg_hbm, wu_hbm)[m].at[j, :, pl.ds(i * width, width)]
        return pltpu.make_async_copy(
            source, wbuf.at[slot, :, cols], l_sem.at[j - n_part]
        )

    down_at, at = {}, n_late * width
    for n, (_, c) in enumerate(steps):
        for j in range(n_local):
            down_at[n, j] = at
            at += parts[c][1]

    def down(s, j):
        return place(down_at[s, j], parts[steps[s][1]][1])

    def d_copy(s, j):
        k, c = steps[s]
        slot, cols, _ = down(s, j)
        first, size = parts[c]
        source = wd_hbm.at[j, :, pl.ds(pl.multiple_of(head_of[k] * width + first, LANES), size)]
        return pltpu.make_async_copy(source, wbuf.at[slot, :, cols], d_sem.at[s])

    def load_after(p):
        for j in range(n_part, n_local):
            for m in range(2):
                for i in range(n_exp):
                    if late(j, m, i)[2] == p:
                        late_copy(j, m, i).start()
        for s in range(len(steps)):
            for j in range(n_local):
                if down(s, j)[2] == p:
                    d_copy(s, j).start()

    for c in inputs:
        c.wait()
    stream_bf[...] = stream_ref[...].astype(BF16)
    lane = lax.broadcasted_iota(jnp.int32, (rows, LANES), 1)
    n_experts = wall.shape[2]
    expert_row = lax.broadcasted_iota(jnp.int32, (n_experts, rows), 0)
    dense = jnp.zeros((n_experts, rows), F32)
    for k in range(ids_ref.shape[0]):
        hit = (ids_ref[k : k + 1, :] == expert_row) & (slots_ref[k : k + 1, :] >= 0)
        dense = dense + jnp.where(hit, probs_ref[k : k + 1, :], 0.0)
    wall[0, e] = jnp.zeros((n_experts, LANES), F32)
    wall[0, e, :, :rows] = dense

    @pl.when(mine)
    def _():
        pl.semaphore_wait(barrier, n_exp - 1 + n_head - 1 + 1)

    @pl.when(jnp.logical_not(mine))
    def _():
        pl.semaphore_wait(barrier, n_exp - 1 + n_head - 1 + 2)

    order = list(range(n_exp - 1, 0, -1))
    ctx_c = {
        k: send(ctx_ref, ctx_all.at[e], ctx_s, ctx_r.at[k], on_exp[k]) for k in order
    }
    for k in order:
        ctx_c[k].start()
    stream_c = send(stream_bf, stream_t, st_s, st_r, turned)
    wz_c = [
        send(wall.at[0, e], wall.at[0, e], wz_s, wz_r, on_exp[k])
        for k in range(1, n_exp)
    ]
    proj_c.wait()
    for q in range(2 * n_part):
        w_copy(q).start()
    load_after(-1)

    def prs_c(j):
        i = exp_of[j]
        return send(pbf.at[i], prs.at[h], prs_s, prs_r, {"head": i})

    tile = min(width, 256)
    for group in [[0]] + [order[:1]] + [order[i : i + 2] for i in range(1, len(order), 2)]:
        pieces = []
        for j in group:
            if j:
                ctx_c[j].wait_recv()
            pieces.append(ctx_all[exp_of[j]] if j else ctx_ref[...])
        pieces = jnp.concatenate(pieces, axis=0)
        if group[-1] == order[-1]:

            @pl.when(jnp.logical_not(mine))
            def _():
                stream_c.start()


        def project(i, carry):
            cols = lanes(i, tile)
            part = jnp.dot(pieces, proj[:, cols], preferred_element_type=F32)
            for n, j in enumerate(group):
                mine_part = part[n * rows : (n + 1) * rows]
                pbf[exp_of[j], :, cols] = mine_part.astype(BF16)

                @pl.when(exp_of[j] == h)
                def _():
                    pown[:, cols] = mine_part

            return carry

        lax.fori_loop(0, width // tile, project, 0, unroll=True)
        for j in group:

            @pl.when(exp_of[j] != h)
            def _():
                prs_c(j).start()

    arrived(prs.at[pl.ds(0, n_head - 1)], prs_r)
    attn = pown[...]
    for k in range(1, n_head):
        attn = attn + prs[head_of[k]].astype(F32)
    attn_buf[...] = attn

    @pl.when(jnp.logical_not(mine))
    def _():
        stream_c.wait()

    @pl.when(mine)
    def _():
        stream_t[...] = stream_bf[...]

    attn_c = send(attn_buf, attn_in, at_s, at_r, turned)

    own_cols = lanes(e, width)
    resid = attn + stream_t[...].astype(F32)
    x[0, h, :, own_cols] = (resid * gain_ref[:, own_cols]).astype(BF16)
    square = jnp.sum(resid * resid, axis=1, keepdims=True)
    row_id = lax.broadcasted_iota(jnp.int32, (rows, LANES), 0)
    flat = jnp.sum(jnp.where(row_id == lane, square, 0.0), axis=0, keepdims=True)
    ssq[0, h, e] = jnp.broadcast_to(flat, (8, LANES))

    def x_at(s, k, j):
        return x.at[s, head_of[k], :, lanes(exp_of[j], width)]

    xz_c = {
        j: send(x_at(0, 0, 0), x_at(0, 0, 0), xz_s, xz_r.at[j], on_exp[j])
        for j in range(1, n_exp)
    }
    xh_c = {
        (k, j): send(x_at(0, 0, j), x_at(0, 0, j), xh_s, xh_r.at[k - 1, j], on_head[k])
        for k in range(1, n_head) for j in range(n_exp)
    }
    xt_c = {
        (k, j): send(x_at(0, k, j), x_at(1, k, j), xt_s, xt_r.at[j], on_tok)
        for k in range(n_head) for j in range(n_exp)
    }
    qz_c = [
        send(ssq.at[0, h, e], ssq.at[0, h, e], qz_s, qz_r, on_exp[k])
        for k in range(1, n_exp)
    ]
    qh_c = [
        send(ssq.at[0, h], ssq.at[0, h], qh_s, qh_r, on_head[k])
        for k in range(1, n_head)
    ]
    qt_c = send(ssq.at[0], ssq.at[1], qt_s, qt_r, on_tok)
    wt_c = send(wall.at[0], wall.at[1], wt_s, wt_r, on_tok)

    def forward(j):
        if j >= n_exp:
            return
        if j:
            xz_c[j].wait_recv()
        for k in range(1, n_head):
            xh_c[k, j].start()
        xt_c[0, j].start()

    def share(j):
        if j >= n_exp:
            return
        for k in range(1, n_head):
            xh_c[k, j].wait_recv()
            xt_c[k, j].start()

    def small(p):
        if p == 0:
            arrived(ssq.at[0, 0, pl.ds(0, n_exp - 1)], qz_r)
            for c in qh_c + wz_c:
                c.start()
        if p == max(1, n_exp - 2):
            arrived(ssq.at[0, pl.ds(0, n_head - 1)], qh_r)
            qt_c.start()
            arrived(wall.at[0, pl.ds(0, n_exp - 1)], wz_r)
            wt_c.start()

            @pl.when(jnp.logical_not(mine))
            def _():
                attn_c.start()

    forward(0)
    for j in range(1, n_exp):
        xz_c[j].start()
    for c in qz_c:
        c.start()
    forward(1)
    share(0)
    forward(2)

    token_row = lax.rem(lax.broadcasted_iota(jnp.int32, (tokens, LANES), 0), rows)
    token_lane = lax.broadcasted_iota(jnp.int32, (tokens, LANES), 1)

    def column(value):
        wide = jnp.broadcast_to(value, (n_tok, n_exp, rows, LANES)).reshape(tokens, LANES)
        return jnp.sum(jnp.where(token_row == token_lane, wide, 0.0), axis=1, keepdims=True)

    hid_tile = 256 if n_hid % 256 == 0 else n_hid
    n_tiles = n_hid // hid_tile
    dims = (((1,), (1,)), ((), ()))

    def factors(j):
        sums = column(jnp.sum(ssq[...], axis=2)[:, :, 0:1, :])
        scale = lax.rsqrt(sums / model + eps_value)
        number = (t * n_exp + e) * n_local + j
        expert_of = lax.broadcasted_iota(jnp.int32, wall.shape, 2)
        picked = jnp.where(expert_of == number, wall[...], 0.0)
        return 0.5 * scale, scale * column(jnp.sum(picked, axis=2, keepdims=True))

    def finish(j, i, g, u, scale, factor):
        g = g * scale
        hid[j, :, lanes(i, hid_tile)] = ((g + g * jnp.tanh(g)) * (u * factor)).astype(BF16)

    def up_part(j, p):
        cols = lanes(exp_of[p], width)
        scale, factor = factors(j) if p == n_exp - 1 else (None, None)

        def body(i, carry):
            q = j * n_tiles + i
            span = lanes(i, hid_tile)
            xv = x[:, :, :, cols].reshape(tokens, width)
            g = lax.dot_general(xv, wbuf[2 * j, span, cols], dims, preferred_element_type=F32)
            u = lax.dot_general(xv, wbuf[2 * j + 1, span, cols], dims, preferred_element_type=F32)
            if p:
                g = g + gacc[q]
                u = u + uacc[q]
            if p < n_exp - 1:
                gacc[q] = g
                uacc[q] = u
            else:
                finish(j, i, g, u, scale, factor)
            return carry

        lax.fori_loop(0, n_tiles, body, 0, unroll=True)

    def up_whole(j):
        scale, factor = factors(j)

        def body(i, carry):
            span = lanes(i, hid_tile)
            both = []
            for m in range(2):
                value = jnp.zeros((tokens, hid_tile), F32)
                for n in range(n_exp):
                    slot, cols, _ = late(j, m, n)
                    value = value + lax.dot_general(
                        x[:, :, :, n * width : (n + 1) * width].reshape(tokens, width),
                        wbuf[slot, span, cols], dims, preferred_element_type=F32,
                    )
                both.append(value)
            finish(j, i, both[0], both[1], scale, factor)
            return carry

        lax.fori_loop(0, n_tiles, body, 0, unroll=True)

    for p in range(n_exp):
        arrived(pbf, xt_r.at[p])
        if p == n_exp - 1:
            qt_c.wait_recv()
            wt_c.wait_recv()
        for j in range(n_part):
            if p == 0:
                loaded(wbuf.at[pl.ds(0, 2)], w_sem.at[j])
            up_part(j, p)
            if j == max(0, n_part - 2):
                forward(p + 3)
                share(p + 1)
                small(p)
        load_after(p)
    for j in range(n_part, n_local):
        loaded(wbuf.at[pl.ds(0, 2)], l_sem.at[j - n_part])
        up_whole(j)

    far = n_head - 1
    to_c = [
        send(obf[c].at[k], tin[c].at[k], to_s.at[c], to_r.at[k, c], on_tok) for k, c in steps
    ]
    group = n_exp // 2
    near = lax.div(e, group) * group
    first_of = (near, (n_exp - group) - near)

    def heads_of(c):
        return range(1, n_head) if c else range(1, far)

    def ho_c(k, c, g):
        at = (k - 1, pl.ds(first_of[g], group))
        return send(
            hsend[c].at[at], hrecv[c].at[at], ho_s.at[c], ho_r.at[c, g], on_head[k]
        )

    def zo_c(m, c):
        return send(zsend[c].at[m - 1], zrecv[c].at[m - 1], zo_s.at[c], zo_r.at[c], on_exp[m])

    def heads_arrived(c, g):
        arrived(hrecv[c].at[pl.ds(0, len(heads_of(c))), pl.ds(0, group)], ho_r.at[c, g])

    fz_c = [
        send(fzsend.at[m - 1], fzrecv.at[m - 1], fz_s, fz_r, on_exp[m])
        for m in range(1, n_exp)
    ]
    fh_c = send(fsend, frecv, fh_s, fh_r, on_head[far])

    def head_step(s):
        k, c = steps[s]
        to_c[s].wait_recv()
        if k == far and c == 0:
            for m in range(n_exp - 1, -1, -1):
                i = exp_of[m]
                value = acc[c][s % 4, i] + tin[c][k, i].astype(F32)
                if m:
                    fzsend[m - 1] = value.astype(BF16)
                    fz_c[m - 1].start()
                else:
                    fown[...] = value
        elif k:
            hsend[c][k - 1] = (acc[c][s % 4] + tin[c][k].astype(F32)).astype(BF16)
            for g in (1, 0):
                ho_c(k, c, g).start()
        else:
            own[c][...] = acc[c][s % 4] + tin[c][k].astype(F32)

    def far_step():
        value = fown[...]
        arrived(fzrecv, fz_r)
        for m in range(n_exp - 1, 0, -1):
            value = value + fzrecv[m - 1].astype(F32)
        fsend[...] = value.astype(BF16)
        fh_c.start()

    def summed(m, c):
        value = own[c][exp_of[m]]
        for k in heads_of(c):
            value = value + hrecv[c][k - 1, exp_of[m]].astype(F32)
        return value

    def exp_step(c):
        for m in range(n_exp - 1, 0, -1):
            if m in (n_exp - 1, group - 1):
                heads_arrived(c, m // group)
            zsend[c][m - 1] = summed(m, c).astype(BF16)
            zo_c(m, c).start()

    def down_steps(batch):
        size = parts[steps[batch[0]][1]][1]
        for s in batch:
            loaded(wbuf.at[0, :, pl.ds(0, n_local * size)], d_sem.at[s])
        values = [jnp.zeros((tokens, size), F32) for _ in batch]
        for j in range(n_local):
            for n, s in enumerate(batch):
                slot, cols, _ = down(s, j)
                values[n] = values[n] + jnp.dot(
                    hid[j], wbuf[slot, :, cols], preferred_element_type=F32
                )
        for s, value in zip(batch, values):
            k, c = steps[s]
            value = value.reshape(n_tok, n_exp, rows, size)
            acc[c][s % 4] = value[0]
            obf[c][k] = value[1].astype(BF16)
            to_c[s].start()

    done, s = [], 0
    for b, batch in enumerate(batches):
        down_steps(range(s, s + len(batch)))
        for n in done:
            head_step(n)
        done = range(s, s + len(batch))
        s += len(batch)
        if len(parts) > 2 and b == len(batches) - 2:
            exp_step(0)
            for n in done:
                head_step(n)
            done = ()
    for n in done:
        head_step(n)
    some = pl.ds(0, n_exp - 1)
    sent(ctx_all.at[some], ctx_s)
    sent(pbf.at[some], prs_s)
    sent(pbf.at[some], xz_s)
    sent(x.at[0, pl.ds(0, n_head - 1)], xh_s)
    sent(x.at[0], xt_s)
    sent(ssq.at[0, 0, some], qz_s)
    sent(ssq.at[0, pl.ds(0, n_head - 1)], qh_s)
    sent(wall.at[0, some], wz_s)
    wt_c.wait_send()
    qt_c.wait_send()
    far_step()
    for c in range(1 if len(parts) > 2 else 0, len(parts)):
        exp_step(c)

    @pl.when(jnp.logical_not(mine))
    def _():
        attn_c.wait()

    @pl.when(mine)
    def _():
        attn_in[...] = attn_buf[...]

    for c, (first, size) in enumerate(parts):
        if group == 1:
            heads_arrived(c, 0)
        value = summed(0, c) + attn_in[:, first : first + size]
        if c == 0:
            fh_c.wait_recv()
            value = value + frecv[...].astype(F32)
        arrived(zrecv[c], zo_r.at[c])
        for m in range(n_exp - 1, 0, -1):
            value = value + zrecv[c][m - 1].astype(F32)
        out_ref[:, first : first + size] = value

    for c in range(len(parts)):
        sent(obf[c], to_s.at[c])
        sent(hsend[c].at[pl.ds(0, len(heads_of(c)))], ho_s.at[c])
        sent(zsend[c], zo_s.at[c])
    sent(fzsend, fz_s)
    fh_c.wait_send()


def solution(mesh):
    n_tok, n_head, n_exp = mesh.shape["tok"], mesh.shape["head"], mesh.shape["exp"]

    def on_device(
        context, out_proj, stream, norm_gain, expert_ids, slot_ids, gate_probs, w_gate, w_up, w_down
    ):
        rows, width = stream.shape[1:]
        n_local, n_hid, model = w_gate.shape
        tokens = n_tok * n_exp * rows
        depth = context.shape[2]
        parts = parts_of(width)
        n_parts = len(parts)
        n_steps = sum(len(batch) for batch in batches_of(width, n_head))
        hid_tile = 256 if n_hid % 256 == 0 else n_hid
        n_tiles = n_hid // hid_tile
        n_part = max(1, n_local - 1)
        vmem = pl.BlockSpec(memory_space=pltpu.VMEM)
        hbm = pl.BlockSpec(memory_space=pltpu.HBM)
        dma = pltpu.SemaphoreType.DMA
        V = pltpu.VMEM
        n_slots = max(2 * n_part, 3 * n_local - 2 * n_part)
        scratch = [
            V(context.shape[1:], BF16),
            V((rows, width), F32),
            V((1, model), F32),
            V((expert_ids.shape[2], rows), jnp.int32),
            V((expert_ids.shape[2], rows), jnp.int32),
            V((expert_ids.shape[2], rows), F32),
            dma((6,)),
            V(out_proj.shape, BF16),
            V((n_slots, n_hid, model), BF16),
            V((n_exp, rows, depth), BF16),
            V((n_tok, n_exp, n_tok * n_exp * n_local, LANES), F32),
            V((rows, width), BF16),
            V((rows, width), BF16),
            V((n_exp, rows, width), BF16),
            V((rows, width), F32),
            V((n_head, rows, width), BF16),
            V((rows, width), F32),
            V((rows, width), F32),
            V((n_tok, n_exp, n_exp, 8, LANES), F32),
            V((n_tok, n_exp, rows, model), BF16),
            V((n_part * n_tiles, tokens, hid_tile), F32),
            V((n_part * n_tiles, tokens, hid_tile), F32),
            V((n_local, tokens, n_hid), BF16),
            [V((4, n_exp, rows, size), F32) for _, size in parts],
            [V((n_exp, rows, size), F32) for _, size in parts],
            [V((n_head, n_exp, rows, size), BF16) for _, size in parts],
            [V((n_head, n_exp, rows, size), BF16) for _, size in parts],
            [V((n_head - 1, n_exp, rows, size), BF16) for _, size in parts],
            [V((n_head - 1, n_exp, rows, size), BF16) for _, size in parts],
            [V((n_exp - 1, rows, size), BF16) for _, size in parts],
            [V((n_exp - 1, rows, size), BF16) for _, size in parts],
            V((rows, parts[0][1]), F32),
            V((n_exp - 1, rows, parts[0][1]), BF16),
            V((n_exp - 1, rows, parts[0][1]), BF16),
            V((rows, parts[0][1]), BF16),
            V((rows, parts[0][1]), BF16),
            dma, dma((n_part,)), dma((max(1, n_local - n_part),)), dma((n_steps,)),
            dma, dma((n_exp,)), dma, dma, dma, dma, dma, dma,
            dma, dma, dma, dma,
            dma, dma((n_exp,)), dma, dma, dma, dma((n_head - 1, n_exp)), dma, dma,
            dma, dma((n_exp,)), dma, dma,
            dma((n_parts,)), dma((n_head, n_parts)), dma((n_parts,)), dma((n_parts, 2)),
            dma((n_parts,)), dma((n_parts,)), dma, dma, dma, dma,
        ]
        out = pl.pallas_call(
            functools.partial(kernel, n_tok, n_head, n_exp),
            out_shape=pltpu.VMEM((rows, width), F32),
            in_specs=[hbm] * 10,
            out_specs=vmem,
            scratch_shapes=scratch,
            compiler_params=pltpu.CompilerParams(
                collective_id=0, has_side_effects=True, vmem_limit_bytes=VMEM_BYTES
            ),
        )(
            context[0], out_proj, stream[0], norm_gain[None], expert_ids[0].T, slot_ids[0].T,
            gate_probs[0].T, w_gate, w_up, w_down,
        )
        return stream + out[None]

    in_specs = (
        P("exp", "tok", "head"),
        P("head", "exp"),
        P("exp", "tok", "head"),
        P(),
        P("exp", "tok", None),
        P("exp", "tok", None),
        P("exp", "tok", None),
        P(("tok", "exp"), "head", None),
        P(("tok", "exp"), "head", None),
        P(("tok", "exp"), "head", None),
    )
    return jax.shard_map(
        on_device, mesh=mesh, in_specs=in_specs, out_specs=P("exp", "tok", "head"), check_vma=False
    )
```

```python
import functools

import jax
import jax.numpy as jnp
from jax import lax
from jax.experimental import pallas as pl
from jax.experimental.pallas import tpu as pltpu
from jax.sharding import PartitionSpec as P

MESH = pl.DeviceIdType.MESH
LANES = 128
F32 = jnp.float32
BF16 = jnp.bfloat16
eps_value = 1e-05
VMEM_BYTES = 62_500_000


def parts_of(width):
    sizes = (width // 2, width // 4, width // 4) if width % 512 == 0 else (width // 2, width // 2)
    return [(sum(sizes[:i]), size) for i, size in enumerate(sizes)]


def batches_of(width, n_head):
    parts = parts_of(width)
    far = n_head - 1
    ks = list(range(far - 1, 0, -1)) + [far]
    first = [(k, 0) for k in ks]
    rest = [(k, c) for c in range(1, len(parts) - 1) for k in ks]
    rest += [(k, len(parts) - 1) for k in range(far, 0, -1)]
    own = [(0, c) for c in range(1, len(parts))]

    def cut(steps):
        n = 1 if parts[steps[0][1]][1] > 256 else 2
        return [tuple(steps[i : i + n]) for i in range(0, len(steps), n)]

    others = cut(rest)
    return cut(first) + others[:-1] + [((0, 0),)] + others[-1:] + cut(own)


def partner(a, k):
    out, bit = a, 1
    while bit <= k:
        if k & bit:
            out = out + bit - 2 * bit * lax.rem(lax.div(out, bit), 2)
        bit *= 2
    return out


def kernel(
    n_tok, n_head, n_exp,
    ctx_hbm, proj_hbm, stream_hbm, gain_hbm, ids_hbm, slots_hbm, probs_hbm,
    wg_hbm, wu_hbm, wd_hbm,
    out_ref,
    ctx_ref, stream_ref, gain_ref, ids_ref, slots_ref, probs_ref, in_sem,
    proj, wbuf, ctx_all, wall, stream_bf, stream_t, pbf, pown, prs,
    attn_buf, attn_in, ssq, x, gacc, uacc, hid, acc, own, obf, tin, hsend, hrecv, zsend, zrecv,
    fown, fzsend, fzrecv, fsend, frecv,
    proj_sem, w_sem, l_sem, d_sem, ctx_s, ctx_r, wz_s, wz_r, wt_s, wt_r, st_s, st_r,
    prs_s, prs_r, at_s, at_r, xz_s, xz_r, qz_s, qz_r, xh_s, xh_r, qh_s, qh_r,
    xt_s, xt_r, qt_s, qt_r, to_s, to_r, ho_s, ho_r, zo_s, zo_r, fz_s, fz_r, fh_s, fh_r,
):
    t, h, e = lax.axis_index("tok"), lax.axis_index("head"), lax.axis_index("exp")
    rows, width = stream_ref.shape
    n_local, n_hid, model = wg_hbm.shape
    depth = ctx_ref.shape[1]
    tokens = n_tok * n_exp * rows
    inputs = [
        pltpu.make_async_copy(source, target, in_sem.at[n])
        for n, (source, target) in enumerate((
            (ctx_hbm, ctx_ref), (stream_hbm, stream_ref), (ids_hbm, ids_ref),
            (slots_hbm, slots_ref), (probs_hbm, probs_ref), (gain_hbm, gain_ref),
        ))
    ]
    for c in inputs:
        c.start()
    parts = parts_of(width)
    turned = {"tok": t, "head": e, "exp": h}
    mine = h == e

    def send(src, dst, s_sem, r_sem, device):
        return pltpu.make_async_remote_copy(
            src_ref=src, dst_ref=dst, send_sem=s_sem, recv_sem=r_sem,
            device_id=device, device_id_type=MESH,
        )

    def sent(ref, sem):
        send(ref, ref, sem, sem, {"tok": 1 - t}).wait_send()

    def arrived(ref, sem):
        send(ref, ref, sem, sem, {"tok": 1 - t}).wait_recv()

    def loaded(ref, sem):
        pltpu.make_async_copy(ref, ref, sem).wait()

    exp_of = [partner(e, k) for k in range(n_exp)]
    head_of = [partner(h, k) for k in range(n_head)]
    on_exp = [{"exp": i} for i in exp_of]
    on_head = [{"head": i} for i in head_of]
    on_tok = {"tok": 1 - t}

    barrier = pltpu.get_barrier_semaphore()
    for device in on_exp[1:] + on_head[1:] + [on_tok]:
        pl.semaphore_signal(barrier, inc=1, device_id=device, device_id_type=MESH)

    @pl.when(jnp.logical_not(mine))
    def _():
        pl.semaphore_signal(barrier, inc=1, device_id=turned, device_id_type=MESH)

    def lanes(i, size):
        return pl.ds(pl.multiple_of(i * size, min(size, LANES)), size)

    n_part = max(1, n_local - 1)
    batches = batches_of(width, n_head)
    steps = [step for batch in batches for step in batch]
    proj_c = pltpu.make_async_copy(proj_hbm, proj, proj_sem)
    proj_c.start()

    def w_copy(q):
        source = (wg_hbm, wu_hbm)[q % 2].at[q // 2]
        return pltpu.make_async_copy(source, wbuf.at[q], w_sem.at[q // 2])

    free = [(q, i * width, -1) for q in range(2 * n_part, wbuf.shape[0]) for i in range(n_exp)]
    free += [(q, exp_of[p] * width, p) for p in range(n_exp) for q in range(2 * n_part)]

    def place(at, size):
        slot, first, p = free[at // width]
        return slot, pl.ds(pl.multiple_of(first + at % width, LANES), size), p

    n_late = (n_local - n_part) * 2 * n_exp

    def late(j, m, i):
        return place((((j - n_part) * 2 + m) * n_exp + i) * width, width)

    def late_copy(j, m, i):
        slot, cols, _ = late(j, m, i)
        source = (wg_hbm, wu_hbm)[m].at[j, :, pl.ds(i * width, width)]
        return pltpu.make_async_copy(
            source, wbuf.at[slot, :, cols], l_sem.at[j - n_part]
        )

    down_at, at = {}, n_late * width
    for n, (_, c) in enumerate(steps):
        for j in range(n_local):
            down_at[n, j] = at
            at += parts[c][1]

    def down(s, j):
        return place(down_at[s, j], parts[steps[s][1]][1])

    def d_copy(s, j):
        k, c = steps[s]
        slot, cols, _ = down(s, j)
        first, size = parts[c]
        source = wd_hbm.at[j, :, pl.ds(pl.multiple_of(head_of[k] * width + first, LANES), size)]
        return pltpu.make_async_copy(source, wbuf.at[slot, :, cols], d_sem.at[s])

    def load_after(p):
        for j in range(n_part, n_local):
            for m in range(2):
                for i in range(n_exp):
                    if late(j, m, i)[2] == p:
                        late_copy(j, m, i).start()
        for s in range(len(steps)):
            for j in range(n_local):
                if down(s, j)[2] == p:
                    d_copy(s, j).start()

    for c in inputs:
        c.wait()
    stream_bf[...] = stream_ref[...].astype(BF16)
    lane = lax.broadcasted_iota(jnp.int32, (rows, LANES), 1)
    n_experts = wall.shape[2]
    expert_row = lax.broadcasted_iota(jnp.int32, (n_experts, rows), 0)
    dense = jnp.zeros((n_experts, rows), F32)
    for k in range(ids_ref.shape[0]):
        hit = (ids_ref[k : k + 1, :] == expert_row) & (slots_ref[k : k + 1, :] >= 0)
        dense = dense + jnp.where(hit, probs_ref[k : k + 1, :], 0.0)
    wall[0, e] = jnp.zeros((n_experts, LANES), F32)
    wall[0, e, :, :rows] = dense

    @pl.when(mine)
    def _():
        pl.semaphore_wait(barrier, n_exp - 1 + n_head - 1 + 1)

    @pl.when(jnp.logical_not(mine))
    def _():
        pl.semaphore_wait(barrier, n_exp - 1 + n_head - 1 + 2)

    order = list(range(n_exp - 1, 0, -1))
    ctx_c = {
        k: send(ctx_ref, ctx_all.at[e], ctx_s, ctx_r.at[k], on_exp[k]) for k in order
    }
    for k in order:
        ctx_c[k].start()
    stream_c = send(stream_bf, stream_t, st_s, st_r, turned)
    wz_c = [
        send(wall.at[0, e], wall.at[0, e], wz_s, wz_r, on_exp[k])
        for k in range(1, n_exp)
    ]
    proj_c.wait()
    for q in range(2 * n_part):
        w_copy(q).start()
    load_after(-1)

    def prs_c(j):
        i = exp_of[j]
        return send(pbf.at[i], prs.at[h], prs_s, prs_r, {"head": i})

    tile = min(width, 256)
    for group in [[0]] + [order[:1]] + [order[i : i + 2] for i in range(1, len(order), 2)]:
        pieces = []
        for j in group:
            if j:
                ctx_c[j].wait_recv()
            pieces.append(ctx_all[exp_of[j]] if j else ctx_ref[...])
        pieces = jnp.concatenate(pieces, axis=0)
        if group[-1] == order[-1]:

            @pl.when(jnp.logical_not(mine))
            def _():
                stream_c.start()


        def project(i, carry):
            cols = lanes(i, tile)
            part = jnp.dot(pieces, proj[:, cols], preferred_element_type=F32)
            for n, j in enumerate(group):
                mine_part = part[n * rows : (n + 1) * rows]
                pbf[exp_of[j], :, cols] = mine_part.astype(BF16)

                @pl.when(exp_of[j] == h)
                def _():
                    pown[:, cols] = mine_part

            return carry

        lax.fori_loop(0, width // tile, project, 0, unroll=True)
        for j in group:

            @pl.when(exp_of[j] != h)
            def _():
                prs_c(j).start()

    arrived(prs.at[pl.ds(0, n_head - 1)], prs_r)
    attn = pown[...]
    for k in range(1, n_head):
        attn = attn + prs[head_of[k]].astype(F32)
    attn_buf[...] = attn

    @pl.when(jnp.logical_not(mine))
    def _():
        stream_c.wait()

    @pl.when(mine)
    def _():
        stream_t[...] = stream_bf[...]

    attn_c = send(attn_buf, attn_in, at_s, at_r, turned)

    own_cols = lanes(e, width)
    resid = attn + stream_t[...].astype(F32)
    x[0, h, :, own_cols] = (resid * gain_ref[:, own_cols]).astype(BF16)
    square = jnp.sum(resid * resid, axis=1, keepdims=True)
    row_id = lax.broadcasted_iota(jnp.int32, (rows, LANES), 0)
    flat = jnp.sum(jnp.where(row_id == lane, square, 0.0), axis=0, keepdims=True)
    ssq[0, h, e] = jnp.broadcast_to(flat, (8, LANES))

    def x_at(s, k, j):
        return x.at[s, head_of[k], :, lanes(exp_of[j], width)]

    xz_c = {
        j: send(x_at(0, 0, 0), x_at(0, 0, 0), xz_s, xz_r.at[j], on_exp[j])
        for j in range(1, n_exp)
    }
    xh_c = {
        (k, j): send(x_at(0, 0, j), x_at(0, 0, j), xh_s, xh_r.at[k - 1, j], on_head[k])
        for k in range(1, n_head) for j in range(n_exp)
    }
    xt_c = {
        (k, j): send(x_at(0, k, j), x_at(1, k, j), xt_s, xt_r.at[j], on_tok)
        for k in range(n_head) for j in range(n_exp)
    }
    qz_c = [
        send(ssq.at[0, h, e], ssq.at[0, h, e], qz_s, qz_r, on_exp[k])
        for k in range(1, n_exp)
    ]
    qh_c = [
        send(ssq.at[0, h], ssq.at[0, h], qh_s, qh_r, on_head[k])
        for k in range(1, n_head)
    ]
    qt_c = send(ssq.at[0], ssq.at[1], qt_s, qt_r, on_tok)
    wt_c = send(wall.at[0], wall.at[1], wt_s, wt_r, on_tok)

    def forward(j):
        if j >= n_exp:
            return
        if j:
            xz_c[j].wait_recv()
        for k in range(1, n_head):
            xh_c[k, j].start()
        xt_c[0, j].start()

    def share(j):
        if j >= n_exp:
            return
        for k in range(1, n_head):
            xh_c[k, j].wait_recv()
            xt_c[k, j].start()

    def small(p):
        if p == 0:
            arrived(ssq.at[0, 0, pl.ds(0, n_exp - 1)], qz_r)
            for c in qh_c + wz_c:
                c.start()
        if p == max(1, n_exp - 2):
            arrived(ssq.at[0, pl.ds(0, n_head - 1)], qh_r)
            qt_c.start()
            arrived(wall.at[0, pl.ds(0, n_exp - 1)], wz_r)
            wt_c.start()

            @pl.when(jnp.logical_not(mine))
            def _():
                attn_c.start()

    forward(0)
    for j in range(1, n_exp):
        xz_c[j].start()
    for c in qz_c:
        c.start()
    forward(1)
    share(0)
    forward(2)

    token_row = lax.rem(lax.broadcasted_iota(jnp.int32, (tokens, LANES), 0), rows)
    token_lane = lax.broadcasted_iota(jnp.int32, (tokens, LANES), 1)

    def column(value):
        wide = jnp.broadcast_to(value, (n_tok, n_exp, rows, LANES)).reshape(tokens, LANES)
        return jnp.sum(jnp.where(token_row == token_lane, wide, 0.0), axis=1, keepdims=True)

    hid_tile = 256 if n_hid % 256 == 0 else n_hid
    n_tiles = n_hid // hid_tile
    dims = (((1,), (1,)), ((), ()))

    def factors(j):
        sums = column(jnp.sum(ssq[...], axis=2)[:, :, 0:1, :])
        scale = lax.rsqrt(sums / model + eps_value)
        number = (t * n_exp + e) * n_local + j
        expert_of = lax.broadcasted_iota(jnp.int32, wall.shape, 2)
        picked = jnp.where(expert_of == number, wall[...], 0.0)
        return 0.5 * scale, scale * column(jnp.sum(picked, axis=2, keepdims=True))

    def finish(j, i, g, u, scale, factor):
        g = g * scale
        hid[j, :, lanes(i, hid_tile)] = ((g + g * jnp.tanh(g)) * (u * factor)).astype(BF16)

    def up_part(j, p):
        cols = lanes(exp_of[p], width)
        scale, factor = factors(j) if p == n_exp - 1 else (None, None)

        def body(i, carry):
            q = j * n_tiles + i
            span = lanes(i, hid_tile)
            xv = x[:, :, :, cols].reshape(tokens, width)
            g = lax.dot_general(xv, wbuf[2 * j, span, cols], dims, preferred_element_type=F32)
            u = lax.dot_general(xv, wbuf[2 * j + 1, span, cols], dims, preferred_element_type=F32)
            if p:
                g = g + gacc[q]
                u = u + uacc[q]
            if p < n_exp - 1:
                gacc[q] = g
                uacc[q] = u
            else:
                finish(j, i, g, u, scale, factor)
            return carry

        lax.fori_loop(0, n_tiles, body, 0, unroll=True)

    def up_whole(j):
        scale, factor = factors(j)

        def body(i, carry):
            span = lanes(i, hid_tile)
            both = []
            for m in range(2):
                value = jnp.zeros((tokens, hid_tile), F32)
                for n in range(n_exp):
                    slot, cols, _ = late(j, m, n)
                    value = value + lax.dot_general(
                        x[:, :, :, n * width : (n + 1) * width].reshape(tokens, width),
                        wbuf[slot, span, cols], dims, preferred_element_type=F32,
                    )
                both.append(value)
            finish(j, i, both[0], both[1], scale, factor)
            return carry

        lax.fori_loop(0, n_tiles, body, 0, unroll=True)

    for p in range(n_exp):
        arrived(pbf, xt_r.at[p])
        if p == n_exp - 1:
            qt_c.wait_recv()
            wt_c.wait_recv()
        for j in range(n_part):
            if p == 0:
                loaded(wbuf.at[pl.ds(0, 2)], w_sem.at[j])
            up_part(j, p)
            if j == max(0, n_part - 2):
                forward(p + 3)
                share(p + 1)
                small(p)
        load_after(p)
    for j in range(n_part, n_local):
        loaded(wbuf.at[pl.ds(0, 2)], l_sem.at[j - n_part])
        up_whole(j)

    far, n_first = n_head - 1, len(fown)
    to_c = [
        send(obf[c].at[k], tin[c].at[k], to_s.at[c], to_r.at[k, c], on_tok) for k, c in steps
    ]
    group = n_exp // 2
    near = lax.div(e, group) * group
    first_of = (near, (n_exp - group) - near)

    def heads_of(c):
        return range(1, far) if c < n_first else range(1, n_head)

    def ho_c(k, c, g):
        at = (k - 1, pl.ds(first_of[g], group))
        return send(
            hsend[c].at[at], hrecv[c].at[at], ho_s.at[c], ho_r.at[c, g], on_head[k]
        )

    def zo_c(m, c):
        return send(zsend[c].at[m - 1], zrecv[c].at[m - 1], zo_s.at[c], zo_r.at[c], on_exp[m])

    def heads_arrived(c, g):
        arrived(hrecv[c].at[pl.ds(0, len(heads_of(c))), pl.ds(0, group)], ho_r.at[c, g])

    def fz_c(m, c):
        return send(fzsend[c].at[m - 1], fzrecv[c].at[m - 1], fz_s.at[c], fz_r.at[c], on_exp[m])

    fh_c = [
        send(fsend[c], frecv[c], fh_s.at[c], fh_r.at[c], on_head[far]) for c in range(n_first)
    ]

    def head_step(s):
        k, c = steps[s]
        to_c[s].wait_recv()
        if k == far and c < n_first:
            for m in range(n_exp - 1, -1, -1):
                i = exp_of[m]
                value = acc[c][s % 4, i] + tin[c][k, i].astype(F32)
                if m:
                    fzsend[c][m - 1] = value.astype(BF16)
                    fz_c(m, c).start()
                else:
                    fown[c][...] = value
        elif k:
            hsend[c][k - 1] = (acc[c][s % 4] + tin[c][k].astype(F32)).astype(BF16)
            for g in (1, 0):
                ho_c(k, c, g).start()
        else:
            own[c][...] = acc[c][s % 4] + tin[c][k].astype(F32)

    def far_step(c):
        value = fown[c][...]
        arrived(fzrecv[c], fz_r.at[c])
        for m in range(n_exp - 1, 0, -1):
            value = value + fzrecv[c][m - 1].astype(F32)
        fsend[c][...] = value.astype(BF16)
        fh_c[c].start()

    def summed(m, c):
        value = own[c][exp_of[m]]
        for k in heads_of(c):
            value = value + hrecv[c][k - 1, exp_of[m]].astype(F32)
        return value

    def exp_step(c, g):
        heads_arrived(c, g)
        for m in range((g + 1) * group - 1, max(g * group, 1) - 1, -1):
            zsend[c][m - 1] = summed(m, c).astype(BF16)
            zo_c(m, c).start()

    def down_steps(batch):
        size = parts[steps[batch[0]][1]][1]
        for s in batch:
            loaded(wbuf.at[0, :, pl.ds(0, n_local * size)], d_sem.at[s])
        values = [jnp.zeros((tokens, size), F32) for _ in batch]
        for j in range(n_local):
            for n, s in enumerate(batch):
                slot, cols, _ = down(s, j)
                values[n] = values[n] + jnp.dot(
                    hid[j], wbuf[slot, :, cols], preferred_element_type=F32
                )
        for s, value in zip(batch, values):
            k, c = steps[s]
            value = value.reshape(n_tok, n_exp, rows, size)
            acc[c][s % 4] = value[0]
            obf[c][k] = value[1].astype(BF16)
            to_c[s].start()

    done, s = [], 0
    for b, batch in enumerate(batches):
        down_steps(range(s, s + len(batch)))
        for n in done:
            head_step(n)
        done = range(s, s + len(batch))
        s += len(batch)
        if len(parts) > 2 and b == len(batches) - 2:
            exp_step(0, 1)
            for n in done:
                head_step(n)
            done = ()
        if len(parts) > 2 and b == len(batches) - 1:
            exp_step(0, 0)
    for n in done:
        head_step(n)
    some = pl.ds(0, n_exp - 1)
    sent(ctx_all.at[some], ctx_s)
    sent(pbf.at[some], prs_s)
    sent(pbf.at[some], xz_s)
    sent(x.at[0, pl.ds(0, n_head - 1)], xh_s)
    sent(x.at[0], xt_s)
    sent(ssq.at[0, 0, some], qz_s)
    sent(ssq.at[0, pl.ds(0, n_head - 1)], qh_s)
    sent(wall.at[0, some], wz_s)
    wt_c.wait_send()
    qt_c.wait_send()
    left = range(1 if len(parts) > 2 else 0, len(parts))
    exp_step(left[0], 1)
    for c in range(n_first):
        far_step(c)
    exp_step(left[0], 0)
    for c in left[1:]:
        exp_step(c, 1)
        exp_step(c, 0)

    @pl.when(jnp.logical_not(mine))
    def _():
        attn_c.wait()

    @pl.when(mine)
    def _():
        attn_in[...] = attn_buf[...]

    for c, (first, size) in enumerate(parts):
        value = summed(0, c) + attn_in[:, first : first + size]
        if c < n_first:
            fh_c[c].wait_recv()
            value = value + frecv[c][...].astype(F32)
        arrived(zrecv[c], zo_r.at[c])
        for m in range(n_exp - 1, 0, -1):
            value = value + zrecv[c][m - 1].astype(F32)
        out_ref[:, first : first + size] = value

    for c in range(len(parts)):
        sent(obf[c], to_s.at[c])
        sent(hsend[c].at[pl.ds(0, len(heads_of(c)))], ho_s.at[c])
        sent(zsend[c], zo_s.at[c])
    for c in range(n_first):
        sent(fzsend[c], fz_s.at[c])
        fh_c[c].wait_send()


def solution(mesh):
    n_tok, n_head, n_exp = mesh.shape["tok"], mesh.shape["head"], mesh.shape["exp"]

    def on_device(
        context, out_proj, stream, norm_gain, expert_ids, slot_ids, gate_probs, w_gate, w_up, w_down
    ):
        rows, width = stream.shape[1:]
        n_local, n_hid, model = w_gate.shape
        tokens = n_tok * n_exp * rows
        depth = context.shape[2]
        parts = parts_of(width)
        n_parts = len(parts)
        n_steps = sum(len(batch) for batch in batches_of(width, n_head))
        hid_tile = 256 if n_hid % 256 == 0 else n_hid
        n_tiles = n_hid // hid_tile
        n_part = max(1, n_local - 1)
        vmem = pl.BlockSpec(memory_space=pltpu.VMEM)
        hbm = pl.BlockSpec(memory_space=pltpu.HBM)
        dma = pltpu.SemaphoreType.DMA
        V = pltpu.VMEM
        n_slots = max(2 * n_part, 3 * n_local - 2 * n_part)
        scratch = [
            V(context.shape[1:], BF16),
            V((rows, width), F32),
            V((1, model), F32),
            V((expert_ids.shape[2], rows), jnp.int32),
            V((expert_ids.shape[2], rows), jnp.int32),
            V((expert_ids.shape[2], rows), F32),
            dma((6,)),
            V(out_proj.shape, BF16),
            V((n_slots, n_hid, model), BF16),
            V((n_exp, rows, depth), BF16),
            V((n_tok, n_exp, n_tok * n_exp * n_local, LANES), F32),
            V((rows, width), BF16),
            V((rows, width), BF16),
            V((n_exp, rows, width), BF16),
            V((rows, width), F32),
            V((n_head, rows, width), BF16),
            V((rows, width), F32),
            V((rows, width), F32),
            V((n_tok, n_exp, n_exp, 8, LANES), F32),
            V((n_tok, n_exp, rows, model), BF16),
            V((n_part * n_tiles, tokens, hid_tile), F32),
            V((n_part * n_tiles, tokens, hid_tile), F32),
            V((n_local, tokens, n_hid), BF16),
            [V((4, n_exp, rows, size), F32) for _, size in parts],
            [V((n_exp, rows, size), F32) for _, size in parts],
            [V((n_head, n_exp, rows, size), BF16) for _, size in parts],
            [V((n_head, n_exp, rows, size), BF16) for _, size in parts],
            [V((n_head - 1, n_exp, rows, size), BF16) for _, size in parts],
            [V((n_head - 1, n_exp, rows, size), BF16) for _, size in parts],
            [V((n_exp - 1, rows, size), BF16) for _, size in parts],
            [V((n_exp - 1, rows, size), BF16) for _, size in parts],
            [V((rows, size), F32) for _, size in parts[:-1]],
            [V((n_exp - 1, rows, size), BF16) for _, size in parts[:-1]],
            [V((n_exp - 1, rows, size), BF16) for _, size in parts[:-1]],
            [V((rows, size), BF16) for _, size in parts[:-1]],
            [V((rows, size), BF16) for _, size in parts[:-1]],
            dma, dma((n_part,)), dma((max(1, n_local - n_part),)), dma((n_steps,)),
            dma, dma((n_exp,)), dma, dma, dma, dma, dma, dma,
            dma, dma, dma, dma,
            dma, dma((n_exp,)), dma, dma, dma, dma((n_head - 1, n_exp)), dma, dma,
            dma, dma((n_exp,)), dma, dma,
            dma((n_parts,)), dma((n_head, n_parts)), dma((n_parts,)), dma((n_parts, 2)),
            dma((n_parts,)), dma((n_parts,)),
            dma((n_parts - 1,)), dma((n_parts - 1,)), dma((n_parts - 1,)), dma((n_parts - 1,)),
        ]
        out = pl.pallas_call(
            functools.partial(kernel, n_tok, n_head, n_exp),
            out_shape=pltpu.VMEM((rows, width), F32),
            in_specs=[hbm] * 10,
            out_specs=vmem,
            scratch_shapes=scratch,
            compiler_params=pltpu.CompilerParams(
                collective_id=0, has_side_effects=True, vmem_limit_bytes=VMEM_BYTES
            ),
        )(
            context[0], out_proj, stream[0], norm_gain[None], expert_ids[0].T, slot_ids[0].T,
            gate_probs[0].T, w_gate, w_up, w_down,
        )
        return stream + out[None]

    in_specs = (
        P("exp", "tok", "head"),
        P("head", "exp"),
        P("exp", "tok", "head"),
        P(),
        P("exp", "tok", None),
        P("exp", "tok", None),
        P("exp", "tok", None),
        P(("tok", "exp"), "head", None),
        P(("tok", "exp"), "head", None),
        P(("tok", "exp"), "head", None),
    )
    return jax.shard_map(
        on_device, mesh=mesh, in_specs=in_specs, out_specs=P("exp", "tok", "head"), check_vma=False
    )
```

```python
import functools

import jax
import jax.numpy as jnp
from jax import lax
from jax.experimental import pallas as pl
from jax.experimental.pallas import tpu as pltpu
from jax.sharding import PartitionSpec as P

MESH = pl.DeviceIdType.MESH
LANES = 128
F32 = jnp.float32
BF16 = jnp.bfloat16
eps_value = 1e-05
VMEM_BYTES = 63_000_000


def parts_of(width):
    sizes = (width // 2, width // 4, width // 4) if width % 512 == 0 else (width // 2, width // 2)
    return [(sum(sizes[:i]), size) for i, size in enumerate(sizes)]


def batches_of(width, n_head):
    parts = parts_of(width)
    far = n_head - 1
    ks = list(range(far - 1, 0, -1)) + [far]
    first = [(k, 0) for k in ks]
    rest = [(k, c) for c in range(1, len(parts) - 1) for k in ks]
    rest += [(k, len(parts) - 1) for k in range(far, 0, -1)]
    own = [(0, c) for c in range(1, len(parts))]

    def cut(steps):
        n = 1 if parts[steps[0][1]][1] > 256 else 2
        return [tuple(steps[i : i + n]) for i in range(0, len(steps), n)]

    others = cut(rest)
    return cut(first) + others[:-1] + [((0, 0),)] + others[-1:] + cut(own)


def partner(a, k):
    out, bit = a, 1
    while bit <= k:
        if k & bit:
            out = out + bit - 2 * bit * lax.rem(lax.div(out, bit), 2)
        bit *= 2
    return out


def kernel(
    n_tok, n_head, n_exp,
    ctx_hbm, proj_hbm, stream_hbm, gain_hbm, ids_hbm, slots_hbm, probs_hbm,
    wg_hbm, wu_hbm, wd_hbm,
    out_ref,
    ctx_ref, stream_ref, gain_ref, ids_ref, slots_ref, probs_ref, in_sem,
    proj, wbuf, ctx_all, wall, stream_bf, stream_t, pbf, pown, prs,
    attn_buf, attn_in, ssq, x, gacc, uacc, hid, acc, own, obf, tin, hsend, hrecv, zsend, zrecv,
    fown, fzsend, fzrecv, fsend, frecv,
    proj_sem, w_sem, l_sem, d_sem, ctx_s, ctx_r, wz_s, wz_r, wt_s, wt_r, st_s, st_r,
    prs_s, prs_r, at_s, at_r, xz_s, xz_r, qz_s, qz_r, xh_s, xh_r, qh_s, qh_r,
    xt_s, xt_r, qt_s, qt_r, to_s, to_r, ho_s, ho_r, zo_s, zo_r, fz_s, fz_r, fh_s, fh_r,
):
    t, h, e = lax.axis_index("tok"), lax.axis_index("head"), lax.axis_index("exp")
    rows, width = stream_ref.shape
    n_local, n_hid, model = wg_hbm.shape
    depth = ctx_ref.shape[1]
    tokens = n_tok * n_exp * rows
    inputs = [
        pltpu.make_async_copy(source, target, in_sem.at[n])
        for n, (source, target) in enumerate((
            (ctx_hbm, ctx_ref), (stream_hbm, stream_ref), (ids_hbm, ids_ref),
            (slots_hbm, slots_ref), (probs_hbm, probs_ref), (gain_hbm, gain_ref),
        ))
    ]
    for c in inputs:
        c.start()
    parts = parts_of(width)
    turned = {"tok": t, "head": e, "exp": h}
    mine = h == e

    def send(src, dst, s_sem, r_sem, device):
        return pltpu.make_async_remote_copy(
            src_ref=src, dst_ref=dst, send_sem=s_sem, recv_sem=r_sem,
            device_id=device, device_id_type=MESH,
        )

    def sent(ref, sem):
        send(ref, ref, sem, sem, {"tok": 1 - t}).wait_send()

    def arrived(ref, sem):
        send(ref, ref, sem, sem, {"tok": 1 - t}).wait_recv()

    def loaded(ref, sem):
        pltpu.make_async_copy(ref, ref, sem).wait()

    exp_of = [partner(e, k) for k in range(n_exp)]
    head_of = [partner(h, k) for k in range(n_head)]
    on_exp = [{"exp": i} for i in exp_of]
    on_head = [{"head": i} for i in head_of]
    on_tok = {"tok": 1 - t}

    barrier = pltpu.get_barrier_semaphore()
    for device in on_exp[1:] + on_head[1:] + [on_tok]:
        pl.semaphore_signal(barrier, inc=1, device_id=device, device_id_type=MESH)

    @pl.when(jnp.logical_not(mine))
    def _():
        pl.semaphore_signal(barrier, inc=1, device_id=turned, device_id_type=MESH)

    def lanes(i, size):
        return pl.ds(pl.multiple_of(i * size, min(size, LANES)), size)

    n_part = max(1, n_local - 1)
    batches = batches_of(width, n_head)
    steps = [step for batch in batches for step in batch]
    proj_c = pltpu.make_async_copy(proj_hbm, proj, proj_sem)
    proj_c.start()

    def w_copy(q):
        source = (wg_hbm, wu_hbm)[q % 2].at[q // 2]
        return pltpu.make_async_copy(source, wbuf.at[q], w_sem.at[q // 2])

    free = [(q, i * width, -1) for q in range(2 * n_part, wbuf.shape[0]) for i in range(n_exp)]
    free += [(q, exp_of[p] * width, p) for p in range(n_exp) for q in range(2 * n_part)]

    def place(at, size):
        slot, first, p = free[at // width]
        return slot, pl.ds(pl.multiple_of(first + at % width, LANES), size), p

    n_late = (n_local - n_part) * 2 * n_exp

    def late(j, m, i):
        return place((((j - n_part) * 2 + m) * n_exp + i) * width, width)

    def late_copy(j, m, i):
        slot, cols, _ = late(j, m, i)
        source = (wg_hbm, wu_hbm)[m].at[j, :, pl.ds(i * width, width)]
        return pltpu.make_async_copy(
            source, wbuf.at[slot, :, cols], l_sem.at[j - n_part]
        )

    down_at, at = {}, n_late * width
    for n, (_, c) in enumerate(steps):
        for j in range(n_local):
            down_at[n, j] = at
            at += parts[c][1]

    def down(s, j):
        return place(down_at[s, j], parts[steps[s][1]][1])

    def d_copy(s, j):
        k, c = steps[s]
        slot, cols, _ = down(s, j)
        first, size = parts[c]
        source = wd_hbm.at[j, :, pl.ds(pl.multiple_of(head_of[k] * width + first, LANES), size)]
        return pltpu.make_async_copy(source, wbuf.at[slot, :, cols], d_sem.at[s])

    def load_after(p):
        for j in range(n_part, n_local):
            for m in range(2):
                for i in range(n_exp):
                    if late(j, m, i)[2] == p:
                        late_copy(j, m, i).start()
        for s in range(len(steps)):
            for j in range(n_local):
                if down(s, j)[2] == p:
                    d_copy(s, j).start()

    for c in inputs:
        c.wait()
    stream_bf[...] = stream_ref[...].astype(BF16)
    lane = lax.broadcasted_iota(jnp.int32, (rows, LANES), 1)
    n_experts = wall.shape[2]
    expert_row = lax.broadcasted_iota(jnp.int32, (n_experts, rows), 0)
    dense = jnp.zeros((n_experts, rows), F32)
    for k in range(ids_ref.shape[0]):
        hit = (ids_ref[k : k + 1, :] == expert_row) & (slots_ref[k : k + 1, :] >= 0)
        dense = dense + jnp.where(hit, probs_ref[k : k + 1, :], 0.0)
    wall[0, e] = jnp.zeros((n_experts, LANES), F32)
    wall[0, e, :, :rows] = dense

    @pl.when(mine)
    def _():
        pl.semaphore_wait(barrier, n_exp - 1 + n_head - 1 + 1)

    @pl.when(jnp.logical_not(mine))
    def _():
        pl.semaphore_wait(barrier, n_exp - 1 + n_head - 1 + 2)

    order = list(range(n_exp - 1, 0, -1))
    ctx_c = {
        k: send(ctx_ref, ctx_all.at[e], ctx_s, ctx_r.at[k], on_exp[k]) for k in order
    }
    for k in order:
        ctx_c[k].start()
    stream_c = send(stream_bf, stream_t, st_s, st_r, turned)
    wz_c = [
        send(wall.at[0, e], wall.at[0, e], wz_s, wz_r, on_exp[k])
        for k in range(1, n_exp)
    ]
    proj_c.wait()
    for q in range(2 * n_part):
        w_copy(q).start()
    load_after(-1)

    def prs_c(j):
        i = exp_of[j]
        return send(pbf.at[i], prs.at[h], prs_s, prs_r, {"head": i})

    tile = min(width, 256)
    for group in [[0]] + [order[:1]] + [order[i : i + 2] for i in range(1, len(order), 2)]:
        pieces = []
        for j in group:
            if j:
                ctx_c[j].wait_recv()
            pieces.append(ctx_all[exp_of[j]] if j else ctx_ref[...])
        pieces = jnp.concatenate(pieces, axis=0)
        if group[-1] == order[-1]:

            @pl.when(jnp.logical_not(mine))
            def _():
                stream_c.start()


        def project(i, carry):
            cols = lanes(i, tile)
            part = jnp.dot(pieces, proj[:, cols], preferred_element_type=F32)
            for n, j in enumerate(group):
                piece = part[n * rows : (n + 1) * rows]
                pbf[exp_of[j], :, cols] = piece.astype(BF16)
                pown[exp_of[j], :, cols] = piece
            return carry

        lax.fori_loop(0, width // tile, project, 0, unroll=True)
        for j in group:

            @pl.when(exp_of[j] != h)
            def _():
                prs_c(j).start()

    arrived(prs.at[pl.ds(0, n_head - 1)], prs_r)
    attn = pown[h]
    for k in range(1, n_head):
        attn = attn + prs[head_of[k]].astype(F32)
    attn_buf[...] = attn

    @pl.when(jnp.logical_not(mine))
    def _():
        stream_c.wait()

    @pl.when(mine)
    def _():
        stream_t[...] = stream_bf[...]

    attn_c = send(attn_buf, attn_in, at_s, at_r, turned)

    own_cols = lanes(e, width)
    resid = attn + stream_t[...].astype(F32)
    x[0, h, :, own_cols] = (resid * gain_ref[:, own_cols]).astype(BF16)
    def x_at(s, k, j):
        return x.at[s, head_of[k], :, lanes(exp_of[j], width)]

    xz_c = {
        j: send(x_at(0, 0, 0), x_at(0, 0, 0), xz_s, xz_r.at[j], on_exp[j])
        for j in range(1, n_exp)
    }
    xh_c = {
        (k, j): send(x_at(0, 0, j), x_at(0, 0, j), xh_s, xh_r.at[k - 1, j], on_head[k])
        for k in range(1, n_head) for j in range(n_exp)
    }
    xt_c = {
        (k, j): send(x_at(0, k, j), x_at(1, k, j), xt_s, xt_r.at[j], on_tok)
        for k in range(n_head) for j in range(n_exp)
    }
    qz_c = [
        send(ssq.at[0, h, e], ssq.at[0, h, e], qz_s, qz_r, on_exp[k])
        for k in range(1, n_exp)
    ]
    qh_c = [
        send(ssq.at[0, h], ssq.at[0, h], qh_s, qh_r, on_head[k])
        for k in range(1, n_head)
    ]
    qt_c = send(ssq.at[0], ssq.at[1], qt_s, qt_r, on_tok)
    wt_c = send(wall.at[0], wall.at[1], wt_s, wt_r, on_tok)

    def forward(j):
        if j >= n_exp:
            return
        if j:
            xz_c[j].wait_recv()
        for k in range(1, n_head):
            xh_c[k, j].start()
        xt_c[0, j].start()

    def share(j):
        if j >= n_exp:
            return
        for k in range(1, n_head):
            xh_c[k, j].wait_recv()
            xt_c[k, j].start()

    def small(p):
        if p == 0:
            arrived(ssq.at[0, 0, pl.ds(0, n_exp - 1)], qz_r)
            for c in qh_c + wz_c:
                c.start()
        if p == max(1, n_exp - 2):
            arrived(ssq.at[0, pl.ds(0, n_head - 1)], qh_r)
            qt_c.start()
            arrived(wall.at[0, pl.ds(0, n_exp - 1)], wz_r)
            wt_c.start()

            @pl.when(jnp.logical_not(mine))
            def _():
                attn_c.start()

    forward(0)
    for j in range(1, n_exp):
        xz_c[j].start()
    square = jnp.sum(resid * resid, axis=1, keepdims=True)
    row_id = lax.broadcasted_iota(jnp.int32, (rows, LANES), 0)
    flat = jnp.sum(jnp.where(row_id == lane, square, 0.0), axis=0, keepdims=True)
    ssq[0, h, e] = jnp.broadcast_to(flat, (8, LANES))
    for c in qz_c:
        c.start()
    forward(1)
    share(0)
    forward(2)

    token_row = lax.rem(lax.broadcasted_iota(jnp.int32, (tokens, LANES), 0), rows)
    token_lane = lax.broadcasted_iota(jnp.int32, (tokens, LANES), 1)

    def column(value):
        wide = jnp.broadcast_to(value, (n_tok, n_exp, rows, LANES)).reshape(tokens, LANES)
        return jnp.sum(jnp.where(token_row == token_lane, wide, 0.0), axis=1, keepdims=True)

    hid_tile = 256 if n_hid % 256 == 0 else n_hid
    n_tiles = n_hid // hid_tile
    dims = (((1,), (1,)), ((), ()))

    def factors(j):
        sums = column(jnp.sum(ssq[...], axis=2)[:, :, 0:1, :])
        scale = lax.rsqrt(sums / model + eps_value)
        number = (t * n_exp + e) * n_local + j
        expert_of = lax.broadcasted_iota(jnp.int32, wall.shape, 2)
        picked = jnp.where(expert_of == number, wall[...], 0.0)
        return 0.5 * scale, scale * column(jnp.sum(picked, axis=2, keepdims=True))

    def finish(j, i, g, u, scale, factor):
        g = g * scale
        hid[j, :, lanes(i, hid_tile)] = ((g + g * jnp.tanh(g)) * (u * factor)).astype(BF16)

    def up_part(j, p):
        cols = lanes(exp_of[p], width)
        scale, factor = factors(j) if p == n_exp - 1 else (None, None)

        def body(i, carry):
            q = j * n_tiles + i
            span = lanes(i, hid_tile)
            xv = x[:, :, :, cols].reshape(tokens, width)
            g = lax.dot_general(xv, wbuf[2 * j, span, cols], dims, preferred_element_type=F32)
            u = lax.dot_general(xv, wbuf[2 * j + 1, span, cols], dims, preferred_element_type=F32)
            if p:
                g = g + gacc[q]
                u = u + uacc[q]
            if p < n_exp - 1:
                gacc[q] = g
                uacc[q] = u
            else:
                finish(j, i, g, u, scale, factor)
            return carry

        lax.fori_loop(0, n_tiles, body, 0, unroll=True)

    def up_whole(j):
        scale, factor = factors(j)

        def body(i, carry):
            span = lanes(i, hid_tile)
            both = []
            for m in range(2):
                value = jnp.zeros((tokens, hid_tile), F32)
                for n in range(n_exp):
                    slot, cols, _ = late(j, m, n)
                    value = value + lax.dot_general(
                        x[:, :, :, n * width : (n + 1) * width].reshape(tokens, width),
                        wbuf[slot, span, cols], dims, preferred_element_type=F32,
                    )
                both.append(value)
            finish(j, i, both[0], both[1], scale, factor)
            return carry

        lax.fori_loop(0, n_tiles, body, 0, unroll=True)

    for p in range(n_exp):
        arrived(pbf, xt_r.at[p])
        if p == n_exp - 1:
            qt_c.wait_recv()
            wt_c.wait_recv()
        for j in range(n_part):
            if p == 0:
                loaded(wbuf.at[pl.ds(0, 2)], w_sem.at[j])
            up_part(j, p)
            if j == max(0, n_part - 2):
                forward(p + 3)
                share(p + 1)
                small(p)
        load_after(p)
    for j in range(n_part, n_local):
        loaded(wbuf.at[pl.ds(0, 2)], l_sem.at[j - n_part])
        up_whole(j)

    far, n_first = n_head - 1, len(fown)
    to_c = [
        send(obf[c].at[k], tin[c].at[k], to_s.at[c], to_r.at[k, c], on_tok) for k, c in steps
    ]
    group = n_exp // 2
    near = lax.div(e, group) * group
    first_of = (near, (n_exp - group) - near)

    def heads_of(c):
        return range(1, far) if c < n_first else range(1, n_head)

    def ho_c(k, c, g):
        at = (k - 1, pl.ds(first_of[g], group))
        return send(
            hsend[c].at[at], hrecv[c].at[at], ho_s.at[c], ho_r.at[c, g], on_head[k]
        )

    def zo_c(m, c):
        return send(zsend[c].at[m - 1], zrecv[c].at[m - 1], zo_s.at[c], zo_r.at[c], on_exp[m])

    def heads_arrived(c, g):
        arrived(hrecv[c].at[pl.ds(0, len(heads_of(c))), pl.ds(0, group)], ho_r.at[c, g])

    def fz_c(m, c):
        return send(fzsend[c].at[m - 1], fzrecv[c].at[m - 1], fz_s.at[c], fz_r.at[c], on_exp[m])

    fh_c = [
        send(fsend[c], frecv[c], fh_s.at[c], fh_r.at[c], on_head[far]) for c in range(n_first)
    ]

    def head_step(s):
        k, c = steps[s]
        to_c[s].wait_recv()
        if k == far and c < n_first:
            for m in range(n_exp - 1, -1, -1):
                i = exp_of[m]
                value = acc[c][s % 4, i] + tin[c][k, i].astype(F32)
                if m:
                    fzsend[c][m - 1] = value.astype(BF16)
                    fz_c(m, c).start()
                else:
                    fown[c][...] = value
        elif k:
            hsend[c][k - 1] = (acc[c][s % 4] + tin[c][k].astype(F32)).astype(BF16)
            for g in (1, 0):
                ho_c(k, c, g).start()
        else:
            own[c][...] = acc[c][s % 4] + tin[c][k].astype(F32)

    def far_step(c):
        value = fown[c][...]
        arrived(fzrecv[c], fz_r.at[c])
        for m in range(n_exp - 1, 0, -1):
            value = value + fzrecv[c][m - 1].astype(F32)
        fsend[c][...] = value.astype(BF16)
        fh_c[c].start()

    def summed(m, c):
        value = own[c][exp_of[m]]
        for k in heads_of(c):
            value = value + hrecv[c][k - 1, exp_of[m]].astype(F32)
        return value

    def exp_step(c, g):
        heads_arrived(c, g)
        for m in range((g + 1) * group - 1, max(g * group, 1) - 1, -1):
            zsend[c][m - 1] = summed(m, c).astype(BF16)
            zo_c(m, c).start()

    def down_steps(batch):
        size = parts[steps[batch[0]][1]][1]
        for s in batch:
            loaded(wbuf.at[0, :, pl.ds(0, n_local * size)], d_sem.at[s])
        values = [jnp.zeros((tokens, size), F32) for _ in batch]
        for j in range(n_local):
            for n, s in enumerate(batch):
                slot, cols, _ = down(s, j)
                values[n] = values[n] + jnp.dot(
                    hid[j], wbuf[slot, :, cols], preferred_element_type=F32
                )
        for s, value in zip(batch, values):
            k, c = steps[s]
            value = value.reshape(n_tok, n_exp, rows, size)
            acc[c][s % 4] = value[0]
            obf[c][k] = value[1].astype(BF16)
            to_c[s].start()

    done, s = [], 0
    for b, batch in enumerate(batches):
        down_steps(range(s, s + len(batch)))
        for n in done:
            head_step(n)
        done = range(s, s + len(batch))
        s += len(batch)
        if len(parts) > 2 and b == len(batches) - 2:
            exp_step(0, 1)
            for n in done:
                head_step(n)
            done = ()
        if len(parts) > 2 and b == len(batches) - 1:
            exp_step(0, 0)
    for n in done:
        head_step(n)
    some = pl.ds(0, n_exp - 1)
    sent(ctx_all.at[some], ctx_s)
    sent(pbf.at[some], prs_s)
    sent(pbf.at[some], xz_s)
    sent(x.at[0, pl.ds(0, n_head - 1)], xh_s)
    sent(x.at[0], xt_s)
    sent(ssq.at[0, 0, some], qz_s)
    sent(ssq.at[0, pl.ds(0, n_head - 1)], qh_s)
    sent(wall.at[0, some], wz_s)
    wt_c.wait_send()
    qt_c.wait_send()
    left = range(1 if len(parts) > 2 else 0, len(parts))
    exp_step(left[0], 1)
    for c in range(n_first):
        far_step(c)
    exp_step(left[0], 0)
    for c in left[1:]:
        exp_step(c, 1)
        exp_step(c, 0)

    @pl.when(jnp.logical_not(mine))
    def _():
        attn_c.wait()

    @pl.when(mine)
    def _():
        attn_in[...] = attn_buf[...]

    for c, (first, size) in enumerate(parts):
        value = summed(0, c) + attn_in[:, first : first + size]
        if c < n_first:
            fh_c[c].wait_recv()
            value = value + frecv[c][...].astype(F32)
        arrived(zrecv[c], zo_r.at[c])
        for m in range(n_exp - 1, 0, -1):
            value = value + zrecv[c][m - 1].astype(F32)
        out_ref[:, first : first + size] = value

    for c in range(len(parts)):
        sent(obf[c], to_s.at[c])
        sent(hsend[c].at[pl.ds(0, len(heads_of(c)))], ho_s.at[c])
        sent(zsend[c], zo_s.at[c])
    for c in range(n_first):
        sent(fzsend[c], fz_s.at[c])
        fh_c[c].wait_send()


def solution(mesh):
    n_tok, n_head, n_exp = mesh.shape["tok"], mesh.shape["head"], mesh.shape["exp"]

    def on_device(
        context, out_proj, stream, norm_gain, expert_ids, slot_ids, gate_probs, w_gate, w_up, w_down
    ):
        rows, width = stream.shape[1:]
        n_local, n_hid, model = w_gate.shape
        tokens = n_tok * n_exp * rows
        depth = context.shape[2]
        parts = parts_of(width)
        n_parts = len(parts)
        n_steps = sum(len(batch) for batch in batches_of(width, n_head))
        hid_tile = 256 if n_hid % 256 == 0 else n_hid
        n_tiles = n_hid // hid_tile
        n_part = max(1, n_local - 1)
        vmem = pl.BlockSpec(memory_space=pltpu.VMEM)
        hbm = pl.BlockSpec(memory_space=pltpu.HBM)
        dma = pltpu.SemaphoreType.DMA
        V = pltpu.VMEM
        n_slots = max(2 * n_part, 3 * n_local - 2 * n_part)
        scratch = [
            V(context.shape[1:], BF16),
            V((rows, width), F32),
            V((1, model), F32),
            V((expert_ids.shape[2], rows), jnp.int32),
            V((expert_ids.shape[2], rows), jnp.int32),
            V((expert_ids.shape[2], rows), F32),
            dma((6,)),
            V(out_proj.shape, BF16),
            V((n_slots, n_hid, model), BF16),
            V((n_exp, rows, depth), BF16),
            V((n_tok, n_exp, n_tok * n_exp * n_local, LANES), F32),
            V((rows, width), BF16),
            V((rows, width), BF16),
            V((n_exp, rows, width), BF16),
            V((n_exp, rows, width), F32),
            V((n_head, rows, width), BF16),
            V((rows, width), F32),
            V((rows, width), F32),
            V((n_tok, n_exp, n_exp, 8, LANES), F32),
            V((n_tok, n_exp, rows, model), BF16),
            V((n_part * n_tiles, tokens, hid_tile), F32),
            V((n_part * n_tiles, tokens, hid_tile), F32),
            V((n_local, tokens, n_hid), BF16),
            [V((4, n_exp, rows, size), F32) for _, size in parts],
            [V((n_exp, rows, size), F32) for _, size in parts],
            [V((n_head, n_exp, rows, size), BF16) for _, size in parts],
            [V((n_head, n_exp, rows, size), BF16) for _, size in parts],
            [V((n_head - 1, n_exp, rows, size), BF16) for _, size in parts],
            [V((n_head - 1, n_exp, rows, size), BF16) for _, size in parts],
            [V((n_exp - 1, rows, size), BF16) for _, size in parts],
            [V((n_exp - 1, rows, size), BF16) for _, size in parts],
            [V((rows, size), F32) for _, size in parts[:-1]],
            [V((n_exp - 1, rows, size), BF16) for _, size in parts[:-1]],
            [V((n_exp - 1, rows, size), BF16) for _, size in parts[:-1]],
            [V((rows, size), BF16) for _, size in parts[:-1]],
            [V((rows, size), BF16) for _, size in parts[:-1]],
            dma, dma((n_part,)), dma((max(1, n_local - n_part),)), dma((n_steps,)),
            dma, dma((n_exp,)), dma, dma, dma, dma, dma, dma,
            dma, dma, dma, dma,
            dma, dma((n_exp,)), dma, dma, dma, dma((n_head - 1, n_exp)), dma, dma,
            dma, dma((n_exp,)), dma, dma,
            dma((n_parts,)), dma((n_head, n_parts)), dma((n_parts,)), dma((n_parts, 2)),
            dma((n_parts,)), dma((n_parts,)),
            dma((n_parts - 1,)), dma((n_parts - 1,)), dma((n_parts - 1,)), dma((n_parts - 1,)),
        ]
        out = pl.pallas_call(
            functools.partial(kernel, n_tok, n_head, n_exp),
            out_shape=pltpu.VMEM((rows, width), F32),
            in_specs=[hbm] * 10,
            out_specs=vmem,
            scratch_shapes=scratch,
            compiler_params=pltpu.CompilerParams(
                collective_id=0, has_side_effects=True, vmem_limit_bytes=VMEM_BYTES
            ),
        )(
            context[0], out_proj, stream[0], norm_gain[None], expert_ids[0].T, slot_ids[0].T,
            gate_probs[0].T, w_gate, w_up, w_down,
        )
        return stream + out[None]

    in_specs = (
        P("exp", "tok", "head"),
        P("head", "exp"),
        P("exp", "tok", "head"),
        P(),
        P("exp", "tok", None),
        P("exp", "tok", None),
        P("exp", "tok", None),
        P(("tok", "exp"), "head", None),
        P(("tok", "exp"), "head", None),
        P(("tok", "exp"), "head", None),
    )
    return jax.shard_map(
        on_device, mesh=mesh, in_specs=in_specs, out_specs=P("exp", "tok", "head"), check_vma=False
    )
```
